32 devices in a mesh: depth: 4 (over x, core), tile: 8 (over z, y).
Axes of the slice: x: 2, y: 2, z: 4, core: 2. Of those that a mesh axis runs over, the one named last changes fastest.
Arguments:
- potential: float32 [3, 256, 256, 512], P(None, 'depth', 'tile'), may hold values from -6 to 6
- channel_index: int32 [64], replicated, may hold values from 0 to 63, each once
- patch_offsets: int32 [3], replicated, may hold values from 0 to 4095
Outputs:
- pol_spectra: float32 [64, 2, 256, 512], P('depth', None, 'tile')
- faraday_depth: float32 [256, 512], P('tile')
The draws below stay inside these ranges and needn't reach their ends.
Inputs may be any that keep to these rules, and one draw needn't show every extreme that they name: `channel_index`: every channel index appears once.
All inputs are finite; a program needn't handle non-finite values.
Results may differ from the reference program's by a relative error of at most 0.00002.
Values sent between devices are 32-bit elements; how exact they have to be, the bound alone decides.
A program may use at most 256 MiB of HBM per device.

```python
import jax
import jax.numpy as jnp
from jax import lax

NY = 512
NCH = 64
NZ = 256
NX = 256


def block_scale(stream_key, extent, cuts, least, largest):
    def one(position, parts):
        heights = jax.random.uniform(jax.random.fold_in(jax.random.fold_in(stream_key, 6), position), (parts,), jnp.float32, least / len(cuts), largest / len(cuts))
        return jnp.repeat(jnp.exp(heights), extent[position] // parts).reshape((-1,) + (1,) * (len(extent) - position - 1))

    factor_of = one(*cuts[0])
    for cut in cuts[1:]:
        factor_of = factor_of * one(*cut)
    return factor_of


def noise(own_key, dims, spread, reach, shards=(), kind=jnp.bfloat16):
    entries = spread * jax.random.normal(own_key, dims, jnp.float32)
    if shards:
        entries = entries * block_scale(own_key, dims, shards, -0.22, 0.18)
    return jnp.clip(entries, -reach, reach).astype(kind)


def setup_inputs(seed: int = 0) -> dict:
    keys = jax.random.split(jax.random.key(seed), 4)
    potential = noise(keys[0], (3, NZ, NX, NY), 1.0, 6.0, ((1, 4), (2, 8)), jnp.float32)
    channel_index = jax.random.permutation(keys[1], NCH).astype(jnp.int32)
    patch_offsets = jax.random.randint(keys[2], (3,), 0, 4096).astype(jnp.int32)
    return dict(potential=potential, channel_index=channel_index, patch_offsets=patch_offsets)


two_pi = 6.283185307179586
faraday_coef = 0.25

def deriv(padded, axis):
    count = padded.shape[axis] - 4

    def take(start):
        return lax.slice_in_dim(padded, start, start + count, axis=axis)
    result = (8.0 * (take(3) - take(1)) - (take(4) - take(0))) / 12.0
    for other in range(3):
        if other != axis:
            result = lax.slice_in_dim(result, 2, result.shape[other] - 2, axis=other)
    return result

def reference(potential, channel_index, patch_offsets):
    padded = jnp.pad(potential, ((0, 0), (2, 2), (2, 2), (2, 2)))
    field_x = deriv(padded[2], 2) - deriv(padded[1], 0)
    field_y = deriv(padded[0], 0) - deriv(padded[2], 1)
    field_z = deriv(padded[1], 1) - deriv(padded[0], 2)
    zpos = (jnp.arange(NZ, dtype=jnp.int32) + patch_offsets[0]).astype(jnp.float32)
    xpos = (jnp.arange(NX, dtype=jnp.int32) + patch_offsets[1]).astype(jnp.float32)
    ypos = (jnp.arange(NY, dtype=jnp.int32) + patch_offsets[2]).astype(jnp.float32)
    density = 1.0 + 0.5 * jnp.cos(zpos * (two_pi / 61.0))[:, None, None] * jnp.cos(xpos * (two_pi / 37.0))[None, :, None] + 0.3 * jnp.sin(ypos * (two_pi / 53.0))[None, None, :]
    stokes_q = density * (field_y * field_y - field_x * field_x)
    stokes_u = -2.0 * density * field_x * field_y
    rotation = faraday_coef * jnp.cumsum(density * field_z, axis=0)
    faraday_depth = rotation[-1]
    freq = 0.5 + 1.5 * channel_index.astype(jnp.float32) / (NCH - 1)
    lam2 = (0.2998 / freq) ** 2
    weight = 1.0 / (freq * jnp.sqrt(jnp.float32(NZ)))

    def channel(pair):
        lam, wgt = pair
        phase = 2.0 * lam * rotation
        cosine = jnp.cos(phase)
        sine = jnp.sin(phase)
        real_part = lax.optimization_barrier(jnp.sum(stokes_q * cosine - stokes_u * sine, axis=0)) * wgt
        imag_part = lax.optimization_barrier(jnp.sum(stokes_q * sine + stokes_u * cosine, axis=0)) * wgt
        return jnp.stack([real_part, imag_part], axis=0)
    pol_spectra = lax.map(channel, (lam2, weight))
    return (pol_spectra, faraday_depth)
```

```python
import functools

import jax
import jax.numpy as jnp
import numpy as np
from jax import lax
from jax.experimental import pallas as pl
from jax.experimental.pallas import tpu as pltpu
from jax.sharding import PartitionSpec as P

NCH = 64


two_pi = 6.283185307179586
faraday_coef = 0.25

REACH = 32.0
TERMS = 26


def grid_lam2():
    freq = 0.5 + 1.5 * np.arange(NCH, dtype=np.float64) / (NCH - 1)
    return 2.0 * (0.2998 / freq) ** 2


def series_table():
    lam = grid_lam2()
    middle = 0.5 * (lam.max() + lam.min())
    args = (lam - middle) * REACH
    count = 4096
    theta = (np.arange(count) + 0.5) * (np.pi / count)
    orders = np.arange(TERMS)
    table = np.cos(
        orders[None, :, None] * theta - args[:, None, None] * np.sin(theta)
    ).mean(axis=-1)
    table = table * np.where(orders == 0, 1.0, 2.0)
    table = table * np.where((orders // 2) % 2 == 0, 1.0, -1.0)
    return middle, table.astype(np.float32)


def halves_fit():
    nodes = 0.25 * (np.cos((np.arange(200) + 0.5) * np.pi / 200) + 1.0) / 2.0
    r = np.sqrt(nodes)
    root = np.sqrt(2.0)
    sin_fit = np.polynomial.polynomial.polyfit(nodes, root * np.sin(np.pi * r) / r, 4)
    cos_fit = np.polynomial.polynomial.polyfit(nodes, root * np.cos(np.pi * r), 5)
    return [float(v) for v in sin_fit], [float(v) for v in cos_fit]


SIN_FIT, COS_FIT = halves_fit()


def horner(fit, square):
    total = fit[-1] * square + fit[-2]
    for value in fit[-3::-1]:
        total = total * square + value
    return total


def turn(fraction):
    square = fraction * fraction
    sine = horner(SIN_FIT, square) * fraction
    cosine = horner(COS_FIT, square)
    return 1.0 - sine * sine, sine * cosine


def turn_of_phase(phase):
    laps = jnp.round(phase * (1.0 / two_pi))
    rest = phase - laps * 6.28125
    rest = rest - laps * 0.0019340515136718750
    rest = rest - laps * (two_pi - 6.28125 - 0.0019340515136718750)
    return turn(rest * (1.0 / two_pi))


def field_kernel(zcos, pot, zlow, zhigh, xlow, xhigh, xcos, ysin, q_out, u_out, sum_out):
    slab, strip, width = sum_out.shape
    column = lax.broadcasted_iota(jnp.int32, (strip, width), 1)
    ybase = jnp.broadcast_to(1.0 + 0.3 * ysin[...], (strip, width))
    xhalf = jnp.broadcast_to(0.5 * xcos[...], (strip, width))

    def along_last(v):
        up1 = jnp.where(column < width - 1, pltpu.roll(v, width - 1, 1), 0.0)
        up2 = jnp.where(column < width - 2, pltpu.roll(v, width - 2, 1), 0.0)
        down1 = jnp.where(column >= 1, pltpu.roll(v, 1, 1), 0.0)
        down2 = jnp.where(column >= 2, pltpu.roll(v, 2, 1), 0.0)
        return (8.0 * (up1 - down1) - (up2 - down2)) * (1.0 / 12.0)

    def along_mid(component, z):
        low = xlow[component - 1, z]
        high = xhigh[component - 1, z]
        v = jnp.concatenate([low, pot[component, z], high], axis=0)
        return (8.0 * (v[3 : strip + 3] - v[1 : strip + 1]) - (v[4 : strip + 4] - v[0:strip])) * (
            1.0 / 12.0
        )

    def along_lead(component, z, edge):
        def plane(step):
            if edge is None:
                return pot[component, z + step]
            place = edge + step
            if place < 0:
                return zlow[component, place + 2]
            if place >= slab:
                return zhigh[component, place - slab]
            return pot[component, place]

        return (8.0 * (plane(1) - plane(-1)) - (plane(2) - plane(-2))) * (1.0 / 12.0)

    def one(z, before, edge=None):
        field_x = along_last(pot[2, z]) - along_lead(1, z, edge)
        field_y = along_lead(0, z, edge) - along_mid(2, z)
        field_z = along_mid(1, z) - along_last(pot[0, z])
        density = ybase + zcos[z] * xhalf
        q_out[z] = density * (field_y * field_y - field_x * field_x)
        u_out[z] = -2.0 * density * field_x * field_y
        now = before + density * field_z
        sum_out[z] = now
        return now

    state = jnp.zeros((strip, width), jnp.float32)
    for z in (0, 1):
        state = one(z, state, z)
    state = lax.fori_loop(2, slab - 2, one, state)
    for z in (slab - 2, slab - 1):
        state = one(z, state, z)


def moment_kernel(middle, q_ref, u_ref, sum_ref, start_ref, out):
    slab, strip, width = sum_ref.shape
    group = 8 if slab % 8 == 0 else 1

    def tile(index, carry):
        row = pl.multiple_of((index // (width // 128)) * 8, 8)
        col = pl.multiple_of((index % (width // 128)) * 128, 128)
        place = (pl.ds(row, 8), pl.ds(col, 128))
        start = start_ref[place]
        for j in range(2 * TERMS):
            out[(j,) + place] = jnp.zeros((8, 128), jnp.float32)

        def block(step, carry):
            q_prev, q_now, u_prev, u_now, twice = [], [], [], [], []
            for k in range(group):
                z = step * group + k
                shift = faraday_coef * sum_ref[(z,) + place] + start
                laps = shift * (middle / two_pi)
                cosine, sine = turn(laps - jnp.round(laps))
                q = q_ref[(z,) + place]
                u = u_ref[(z,) + place]
                x = shift * (1.0 / REACH)
                q_prev.append(q * cosine - u * sine)
                u_prev.append(q * sine + u * cosine)
                twice.append(x + x)
                q_now.append(x * q_prev[-1])
                u_now.append(x * u_prev[-1])
            out[(0,) + place] += functools.reduce(jnp.add, q_prev)
            out[(TERMS,) + place] += functools.reduce(jnp.add, u_prev)
            for j in range(1, TERMS):
                out[(j,) + place] += functools.reduce(jnp.add, q_now)
                out[(TERMS + j,) + place] += functools.reduce(jnp.add, u_now)
                if j < TERMS - 1:
                    for k in range(group):
                        q_prev[k], q_now[k] = q_now[k], twice[k] * q_now[k] - q_prev[k]
                        u_prev[k], u_now[k] = u_now[k], twice[k] * u_now[k] - u_prev[k]
            return carry

        return lax.fori_loop(0, slab // group, block, carry)

    lax.fori_loop(0, (strip // 8) * (width // 128), tile, 0)


def channel_kernel(index, lam, weight, table, moments, depth_ref, out):
    rows, _, strip, width = out.shape

    def band(step, carry):
        place = pl.ds(pl.multiple_of(step * 8, 8), 8)
        half = 0.5 * depth_ref[place]

        def one(row, carry):
            base = index[row] * TERMS
            real_part = table[base] * moments[0, place]
            imag_part = table[base] * moments[TERMS, place]
            for j in range(1, TERMS):
                factor = table[base + j]
                first = factor * moments[j, place]
                second = factor * moments[TERMS + j, place]
                if j % 2 == 0:
                    real_part = real_part + first
                    imag_part = imag_part + second
                else:
                    real_part = real_part - second
                    imag_part = imag_part + first
            cosine, sine = turn_of_phase(2.0 * lam[row] * half)
            out[row, 0, place] = (real_part * cosine - imag_part * sine) * weight[row]
            out[row, 1, place] = (real_part * sine + imag_part * cosine) * weight[row]
            return carry

        return lax.fori_loop(0, rows, one, carry)

    lax.fori_loop(0, strip // 8, band, 0)


def direct_kernel(lam, weight, q_ref, u_ref, sum_ref, nearer_ref, out):
    slab, strip, width = sum_ref.shape
    twice = 2.0 * lam[pl.program_id(0)]
    scale = weight[pl.program_id(0)]

    def band(step, carry):
        place = pl.ds(pl.multiple_of(step * 8, 8), 8)
        nearer = nearer_ref[place]

        def one(z, sums):
            cosine, sine = turn_of_phase(twice * (faraday_coef * sum_ref[z, place] + nearer))
            q = q_ref[z, place]
            u = u_ref[z, place]
            return sums[0] + (q * cosine - u * sine), sums[1] + (q * sine + u * cosine)

        zero = jnp.zeros((8, width), jnp.float32)
        real_part, imag_part = lax.fori_loop(0, slab, one, (zero, zero))
        out[0, 0, place] = real_part * scale
        out[0, 1, place] = imag_part * scale
        return carry

    lax.fori_loop(0, strip // 8, band, 0)


vmem = pl.BlockSpec(memory_space=pltpu.VMEM)
smem = pl.BlockSpec(memory_space=pltpu.SMEM)
params = pltpu.CompilerParams(vmem_limit_bytes=60 * 1024 * 1024)


def neighbours(block, axis, dim):
    count = lax.axis_size(axis)
    forward = [(i, i + 1) for i in range(count - 1)]
    backward = [(target, source) for source, target in forward]
    low = lax.ppermute(
        lax.slice_in_dim(block, block.shape[dim] - 2, None, axis=dim), axis, forward
    )
    high = lax.ppermute(lax.slice_in_dim(block, 0, 2, axis=dim), axis, backward)
    return low, high


def body(potential, channel_index, patch_offsets):
    depth_count = lax.axis_size("depth")
    depth_place = lax.axis_index("depth")
    slab, strip, width = (potential.shape[1], potential.shape[2], potential.shape[3])
    zlow, zhigh = neighbours(potential[0:2], "depth", 1)
    xlow, xhigh = neighbours(potential[1:3], "tile", 2)
    zstart = depth_place * slab
    xstart = lax.axis_index("tile") * strip
    zpos = (zstart + jnp.arange(slab, dtype=jnp.int32) + patch_offsets[0]).astype(jnp.float32)
    xpos = (xstart + jnp.arange(strip, dtype=jnp.int32) + patch_offsets[1]).astype(jnp.float32)
    ypos = (jnp.arange(width, dtype=jnp.int32) + patch_offsets[2]).astype(jnp.float32)
    zcos = jnp.cos(zpos * (two_pi / 61.0))
    xcos = jnp.cos(xpos * (two_pi / 37.0))[:, None]
    ysin = jnp.sin(ypos * (two_pi / 53.0))[None, :]
    plane = jax.ShapeDtypeStruct((slab, strip, width), jnp.float32)
    stokes_q, stokes_u, slab_sums = pl.pallas_call(
        field_kernel,
        out_shape=(plane, plane, plane),
        in_specs=[smem] + [vmem] * 7,
        out_specs=(vmem, vmem, vmem),
        compiler_params=params,
    )(zcos, potential, zlow, zhigh, xlow, xhigh, xcos, ysin)

    totals = lax.all_gather(faraday_coef * slab_sums[-1], "depth")
    faraday_depth = jnp.sum(totals, axis=0)
    before = (jnp.arange(depth_count) < depth_place)[:, None, None]
    nearer = jnp.sum(jnp.where(before, totals, 0.0), axis=0)
    start = nearer - 0.5 * faraday_depth

    farthest = jnp.max(jnp.abs(faraday_coef * slab_sums + start[None]))
    farthest = lax.pmax(farthest, ("depth", "tile"))

    middle, table = series_table()
    moments = pl.pallas_call(
        functools.partial(moment_kernel, float(middle)),
        out_shape=jax.ShapeDtypeStruct((2 * TERMS, strip, width), jnp.float32),
        in_specs=[vmem] * 4,
        out_specs=vmem,
        compiler_params=params,
    )(stokes_q, stokes_u, slab_sums, start)
    moments = lax.psum(moments, "depth")

    freq = 0.5 + 1.5 * channel_index.astype(jnp.float32) / (NCH - 1)
    lam2 = (0.2998 / freq) ** 2
    weight = 1.0 / (freq * jnp.sqrt(jnp.float32(slab * depth_count)))
    rows = NCH // depth_count

    def own(values):
        return lax.dynamic_slice_in_dim(values, depth_place * rows, rows)

    def by_series(_):
        return pl.pallas_call(
            channel_kernel,
            out_shape=jax.ShapeDtypeStruct((rows, 2, strip, width), jnp.float32),
            in_specs=[smem] * 4 + [vmem] * 2,
            out_specs=vmem,
            compiler_params=params,
        )(
            own(channel_index),
            own(lam2),
            own(weight),
            jnp.asarray(table.reshape(-1)),
            moments,
            faraday_depth,
        )

    def by_sum(_):
        whole = pl.BlockSpec((slab, strip, width), lambda c: (0, 0, 0))
        sums = pl.pallas_call(
            direct_kernel,
            grid=(NCH,),
            out_shape=jax.ShapeDtypeStruct((NCH, 2, strip, width), jnp.float32),
            in_specs=[smem] * 2
            + [whole] * 3
            + [pl.BlockSpec((strip, width), lambda c: (0, 0))],
            out_specs=pl.BlockSpec((1, 2, strip, width), lambda c: (c, 0, 0, 0)),
            compiler_params=params,
        )(lam2, weight, stokes_q, stokes_u, slab_sums, nearer)
        return lax.psum_scatter(sums, "depth", scatter_dimension=0, tiled=True)

    pol_spectra = lax.cond(farthest <= REACH, by_series, by_sum, 0)
    return (pol_spectra, faraday_depth)


def solution(mesh):
    in_specs = (P(None, "depth", "tile", None), P(), P())
    out_specs = (P("depth", None, "tile", None), P("tile", None))
    return jax.shard_map(body, mesh=mesh, in_specs=in_specs, out_specs=out_specs, check_vma=False)
```

```python
import functools

import jax
import jax.numpy as jnp
import numpy as np
from jax import lax
from jax.experimental import pallas as pl
from jax.experimental.pallas import tpu as pltpu
from jax.sharding import PartitionSpec as P

NCH = 64


two_pi = 6.283185307179586
faraday_coef = 0.25

REACH = 24.0
TERMS = 22


def grid_lam2():
    freq = 0.5 + 1.5 * np.arange(NCH, dtype=np.float64) / (NCH - 1)
    return 2.0 * (0.2998 / freq) ** 2


def series_table():
    lam = grid_lam2()
    middle = 0.5 * (lam.max() + lam.min())
    args = (lam - middle) * REACH
    count = 4096
    theta = (np.arange(count) + 0.5) * (np.pi / count)
    orders = np.arange(TERMS)
    table = np.cos(
        orders[None, :, None] * theta - args[:, None, None] * np.sin(theta)
    ).mean(axis=-1)
    table = table * np.where(orders == 0, 1.0, 2.0)
    table = table * np.where((orders // 2) % 2 == 0, 1.0, -1.0)
    return middle, table.astype(np.float32)


def halves_fit():
    nodes = 0.25 * (np.cos((np.arange(200) + 0.5) * np.pi / 200) + 1.0) / 2.0
    r = np.sqrt(nodes)
    root = np.sqrt(2.0)
    sin_fit = np.polynomial.polynomial.polyfit(nodes, root * np.sin(np.pi * r) / r, 4)
    cos_fit = np.polynomial.polynomial.polyfit(nodes, root * np.cos(np.pi * r), 5)
    return [float(v) for v in sin_fit], [float(v) for v in cos_fit]


SIN_FIT, COS_FIT = halves_fit()


def horner(fit, square):
    total = fit[-1] * square + fit[-2]
    for value in fit[-3::-1]:
        total = total * square + value
    return total


def turn(fraction):
    square = fraction * fraction
    sine = horner(SIN_FIT, square) * fraction
    cosine = horner(COS_FIT, square)
    return 1.0 - sine * sine, sine * cosine


def turn_of_phase(phase):
    laps = jnp.round(phase * (1.0 / two_pi))
    rest = phase - laps * 6.28125
    rest = rest - laps * 0.0019340515136718750
    rest = rest - laps * (two_pi - 6.28125 - 0.0019340515136718750)
    return turn(rest * (1.0 / two_pi))


def field_kernel(zcos, pot, zlow, zhigh, xlow, xhigh, xcos, ysin, q_out, u_out, sum_out, total_out, high_out, low_out):
    slab, strip, width = sum_out.shape
    column = lax.broadcasted_iota(jnp.int32, (strip, width), 1)
    ybase = jnp.broadcast_to(1.0 + 0.3 * ysin[...], (strip, width))
    xhalf = jnp.broadcast_to(0.5 * xcos[...], (strip, width))

    def along_last(v):
        up1 = jnp.where(column < width - 1, pltpu.roll(v, width - 1, 1), 0.0)
        up2 = jnp.where(column < width - 2, pltpu.roll(v, width - 2, 1), 0.0)
        down1 = jnp.where(column >= 1, pltpu.roll(v, 1, 1), 0.0)
        down2 = jnp.where(column >= 2, pltpu.roll(v, 2, 1), 0.0)
        return (8.0 * (up1 - down1) - (up2 - down2)) * (1.0 / 12.0)

    def along_mid(component, z):
        low = xlow[component - 1, z]
        high = xhigh[component - 1, z]
        v = jnp.concatenate([low, pot[component, z], high], axis=0)
        return (8.0 * (v[3 : strip + 3] - v[1 : strip + 1]) - (v[4 : strip + 4] - v[0:strip])) * (
            1.0 / 12.0
        )

    def along_lead(component, z, edge):
        def plane(step):
            if edge is None:
                return pot[component, z + step]
            place = edge + step
            if place < 0:
                return zlow[component, place + 2]
            if place >= slab:
                return zhigh[component, place - slab]
            return pot[component, place]

        return (8.0 * (plane(1) - plane(-1)) - (plane(2) - plane(-2))) * (1.0 / 12.0)

    def one(z, state, edge=None):
        before, high, low = state
        field_x = along_last(pot[2, z]) - along_lead(1, z, edge)
        field_y = along_lead(0, z, edge) - along_mid(2, z)
        field_z = along_mid(1, z) - along_last(pot[0, z])
        density = ybase + zcos[z] * xhalf
        q_out[z] = density * (field_y * field_y - field_x * field_x)
        u_out[z] = -2.0 * density * field_x * field_y
        now = before + density * field_z
        sum_out[z] = now
        return now, jnp.maximum(high, now), jnp.minimum(low, now)

    zero = jnp.zeros((strip, width), jnp.float32)
    state = (zero, zero, zero)
    for z in (0, 1):
        state = one(z, state, z)
    state = lax.fori_loop(2, slab - 2, one, state)
    for z in (slab - 2, slab - 1):
        state = one(z, state, z)
    total_out[...] = faraday_coef * state[0]
    high_out[...] = faraday_coef * state[1]
    low_out[...] = faraday_coef * state[2]


def halo_kernel(zup, zdown, xup, xdown, zlow, zhigh, xlow, xhigh, send, recv):
    barrier = pltpu.get_barrier_semaphore()
    plan = []
    for order, (axis, up, down, low, high) in enumerate(
        (("depth", zup, zdown, zlow, zhigh), ("tile", xup, xdown, xlow, xhigh))
    ):
        place = lax.axis_index(axis)
        last = lax.axis_size(axis) - 1
        above = pltpu.make_async_remote_copy(
            src_ref=up, dst_ref=low, send_sem=send.at[2 * order], recv_sem=recv.at[2 * order],
            device_id={axis: place + 1}, device_id_type=pl.DeviceIdType.MESH,
        )
        below = pltpu.make_async_remote_copy(
            src_ref=down, dst_ref=high, send_sem=send.at[2 * order + 1],
            recv_sem=recv.at[2 * order + 1],
            device_id={axis: place - 1}, device_id_type=pl.DeviceIdType.MESH,
        )
        plan.append((axis, place, last, above, below, low, high))

    def signal(axis, index):
        pl.semaphore_signal(
            barrier, inc=1, device_id={axis: index}, device_id_type=pl.DeviceIdType.MESH
        )

    for axis, place, last, above, below, low, high in plan:
        pl.when(place > 0)(functools.partial(signal, axis, place - 1))
        pl.when(place < last)(functools.partial(signal, axis, place + 1))
    count = 0
    for axis, place, last, above, below, low, high in plan:
        count = count + (place + last - 1) // last + (2 * last - place - 1) // last
    pl.semaphore_wait(barrier, count)
    for axis, place, last, above, below, low, high in reversed(plan):
        pl.when(place < last)(above.start)
        pl.when(place > 0)(below.start)
    for axis, place, last, above, below, low, high in plan:

        @pl.when(place == 0)
        def _():
            low[...] = jnp.zeros_like(low)

        @pl.when(place == last)
        def _():
            high[...] = jnp.zeros_like(high)

    for axis, place, last, above, below, low, high in plan:

        @pl.when(place < last)
        def _():
            above.wait_send()
            below.wait_recv()

        @pl.when(place > 0)
        def _():
            below.wait_send()
            above.wait_recv()


def moment_kernel(
    middle, q_ref, u_ref, sum_ref, total_ref, high_ref, low_ref,
    out, depth_out, far_out,
    others, start_ref, own, near, part, across, far, far_depth, far_mid, far_tile,
    carry_send, carry_recv, far_send, far_recv, tile_send, tile_recv,
    near_send, near_recv, cross_send, cross_recv, back_send, back_recv,
):
    slab, strip, width = sum_ref.shape
    group = 8 if slab % 8 == 0 else 1
    chunks = strip // 8
    depth_count, tile_count = lax.axis_size("depth"), lax.axis_size("tile")
    depth_place, tile_place = lax.axis_index("depth"), lax.axis_index("tile")
    core = lax.rem(depth_place, 2)
    chip_count = depth_count // 2
    chip = depth_place // 2
    partner = depth_place + 1 - 2 * core

    def copy(src, dst, send, recv, axis, index):
        return pltpu.make_async_remote_copy(
            src_ref=src, dst_ref=dst, send_sem=send, recv_sem=recv,
            device_id={axis: index}, device_id_type=pl.DeviceIdType.MESH,
        )

    def depth_peer(k):
        return lax.rem(depth_place + k, depth_count)

    def tile_peer(k):
        return lax.rem(tile_place + k, tile_count)

    barrier = pltpu.get_barrier_semaphore()
    for k in range(1, depth_count):
        pl.semaphore_signal(
            barrier, inc=1, device_id={"depth": depth_peer(k)},
            device_id_type=pl.DeviceIdType.MESH,
        )
    for k in range(1, tile_count):
        pl.semaphore_signal(
            barrier, inc=1, device_id={"tile": tile_peer(k)},
            device_id_type=pl.DeviceIdType.MESH,
        )
    pl.semaphore_wait(barrier, depth_count + tile_count - 2)

    carries = [
        copy(total_ref, others.at[k - 1], carry_send.at[k - 1], carry_recv.at[k - 1],
             "depth", depth_peer(k))
        for k in range(1, depth_count)
    ]
    for item in carries:
        item.start()
    for item in carries:
        item.wait()
    nearer = jnp.zeros((strip, width), jnp.float32)
    whole = total_ref[...]
    for k in range(1, depth_count):
        part_k = others[k - 1]
        whole = whole + part_k
        nearer = nearer + jnp.where(depth_place >= k, part_k, 0.0)
    depth_out[...] = whole
    start = nearer - 0.5 * whole
    start_ref[...] = start
    reach = jnp.maximum(jnp.abs(high_ref[...] + start), jnp.abs(low_ref[...] + start))
    reach = functools.reduce(
        jnp.maximum, [reach[:, k * 128 : (k + 1) * 128] for k in range(width // 128)]
    )
    far[...] = functools.reduce(jnp.maximum, [reach[k * 8 : k * 8 + 8] for k in range(chunks)])
    fars = [
        copy(far, far_depth.at[k - 1], far_send.at[k - 1], far_recv.at[k - 1],
             "depth", depth_peer(k))
        for k in range(1, depth_count)
    ]
    for item in fars:
        item.start()

    def tile(row, col, g):
        rows = pl.ds(pl.multiple_of(row, 8), 8)
        cols = pl.ds(pl.multiple_of(col, 128), 128)
        place = (rows, cols)
        start = start_ref[place]
        for half in range(2):
            for j in range(TERMS):
                own[g, half, j, :, cols] = jnp.zeros((8, 128), jnp.float32)

        def block(step, carry):
            q_prev, q_now, u_prev, u_now, twice = [], [], [], [], []
            for k in range(group):
                z = step * group + k
                shift = faraday_coef * sum_ref[(z,) + place] + start
                laps = shift * (middle / two_pi)
                cosine, sine = turn(laps - jnp.round(laps))
                q = q_ref[(z,) + place]
                u = u_ref[(z,) + place]
                x = shift * (1.0 / REACH)
                q_prev.append(q * cosine - u * sine)
                u_prev.append(q * sine + u * cosine)
                twice.append(x + x)
                q_now.append(x * q_prev[-1])
                u_now.append(x * u_prev[-1])
            own[g, 0, 0, :, cols] += functools.reduce(jnp.add, q_prev)
            own[g, 1, 0, :, cols] += functools.reduce(jnp.add, u_prev)
            for j in range(1, TERMS):
                own[g, 0, j, :, cols] += functools.reduce(jnp.add, q_now)
                own[g, 1, j, :, cols] += functools.reduce(jnp.add, u_now)
                if j < TERMS - 1:
                    for k in range(group):
                        q_prev[k], q_now[k] = q_now[k], twice[k] * q_now[k] - q_prev[k]
                        u_prev[k], u_now[k] = u_now[k], twice[k] * u_now[k] - u_prev[k]
            return carry

        lax.fori_loop(0, slab // group, block, 0)

    def near_copy(g):
        return copy(own.at[g, 1 - core], near.at[g], near_send.at[g], near_recv.at[g],
                    "depth", partner)

    def cross_copies(g):
        return [
            copy(part.at[g], across.at[g, k - 1], cross_send.at[g, k - 1],
                 cross_recv.at[g, k - 1], "depth", 2 * lax.rem(chip + k, chip_count) + core)
            for k in range(1, chip_count)
        ]

    def back_copy(g):
        piece = out.at[core, :, pl.ds(pl.multiple_of(g * 8, 8), 8)]
        return copy(piece, piece, back_send.at[g], back_recv.at[g], "depth", partner)

    def compute(g):
        lax.fori_loop(
            0, width // 128, lambda c, carry: (tile(g * 8, c * 128, g), carry)[1], 0
        )
        near_copy(g).start()

    def sum_chip(g):
        near_copy(g).wait()
        part[g] = own[g, core] + near[g]
        for item in cross_copies(g):
            item.start()

    def sum_all(g):
        total = part[g]
        for k, item in enumerate(cross_copies(g)):
            item.wait()
            total = total + across[g, k]
        out[core, :, pl.ds(pl.multiple_of(g * 8, 8), 8)] = total
        back_copy(g).start()

    tiles_far = [
        copy(far_mid, far_tile.at[k - 1], tile_send.at[k - 1], tile_recv.at[k - 1],
             "tile", tile_peer(k))
        for k in range(1, tile_count)
    ]

    def lap(g, carry):
        pl.when(g < chunks)(lambda: compute(g))

        @pl.when(g == 0)
        def _():
            reach = far[...]
            for k, item in enumerate(fars):
                item.wait()
                reach = jnp.maximum(reach, far_depth[k])
            far_mid[...] = reach
            for item in tiles_far:
                item.start()

        pl.when(jnp.logical_and(g >= 1, g <= chunks))(lambda: sum_chip(g - 1))
        pl.when(g >= 2)(lambda: sum_all(g - 2))
        return carry

    lax.fori_loop(0, chunks + 2, lap, 0)
    reach = far_mid[...]
    for k, item in enumerate(tiles_far):
        item.wait()
        reach = jnp.maximum(reach, far_tile[k])
    far_out[...] = reach
    for g in range(chunks):
        back_copy(g).wait()


def channel_kernel(index, lam, weight, table, moments, depth_ref, out):
    rows, _, strip, width = out.shape

    def band(step, carry):
        place = pl.ds(pl.multiple_of(step * 8, 8), 8)
        half = 0.5 * depth_ref[place]

        def one(row, carry):
            base = index[row] * TERMS
            real_part = table[base] * moments[0, 0, place]
            imag_part = table[base] * moments[1, 0, place]
            for j in range(1, TERMS):
                factor = table[base + j]
                first = factor * moments[0, j, place]
                second = factor * moments[1, j, place]
                if j % 2 == 0:
                    real_part = real_part + first
                    imag_part = imag_part + second
                else:
                    real_part = real_part - second
                    imag_part = imag_part + first
            cosine, sine = turn_of_phase(2.0 * lam[row] * half)
            out[row, 0, place] = (real_part * cosine - imag_part * sine) * weight[row]
            out[row, 1, place] = (real_part * sine + imag_part * cosine) * weight[row]
            return carry

        return lax.fori_loop(0, rows, one, carry)

    lax.fori_loop(0, strip // 8, band, 0)


def direct_kernel(lam, weight, q_ref, u_ref, sum_ref, nearer_ref, out):
    slab, strip, width = sum_ref.shape
    twice = 2.0 * lam[pl.program_id(0)]
    scale = weight[pl.program_id(0)]

    def band(step, carry):
        place = pl.ds(pl.multiple_of(step * 8, 8), 8)
        nearer = nearer_ref[place]

        def one(z, sums):
            cosine, sine = turn_of_phase(twice * (faraday_coef * sum_ref[z, place] + nearer))
            q = q_ref[z, place]
            u = u_ref[z, place]
            return sums[0] + (q * cosine - u * sine), sums[1] + (q * sine + u * cosine)

        zero = jnp.zeros((8, width), jnp.float32)
        real_part, imag_part = lax.fori_loop(0, slab, one, (zero, zero))
        out[0, 0, place] = real_part * scale
        out[0, 1, place] = imag_part * scale
        return carry

    lax.fori_loop(0, strip // 8, band, 0)


vmem = pl.BlockSpec(memory_space=pltpu.VMEM)
smem = pl.BlockSpec(memory_space=pltpu.SMEM)
params = pltpu.CompilerParams(vmem_limit_bytes=60 * 1024 * 1024)


def body(potential, channel_index, patch_offsets):
    depth_count = lax.axis_size("depth")
    depth_place = lax.axis_index("depth")
    slab, strip, width = (potential.shape[1], potential.shape[2], potential.shape[3])
    shapes = [(2, 2, strip, width)] * 2 + [(2, slab, 2, width)] * 2
    zlow, zhigh, xlow, xhigh = pl.pallas_call(
        halo_kernel,
        out_shape=tuple(jax.ShapeDtypeStruct(shape, jnp.float32) for shape in shapes),
        in_specs=[vmem] * 4,
        out_specs=(vmem,) * 4,
        scratch_shapes=[pltpu.SemaphoreType.DMA((4,)), pltpu.SemaphoreType.DMA((4,))],
        compiler_params=pltpu.CompilerParams(collective_id=0, has_side_effects=True),
    )(
        potential[0:2, slab - 2 :],
        potential[0:2, :2],
        potential[1:3, :, strip - 2 :],
        potential[1:3, :, :2],
    )
    zstart = depth_place * slab
    xstart = lax.axis_index("tile") * strip
    zpos = (zstart + jnp.arange(slab, dtype=jnp.int32) + patch_offsets[0]).astype(jnp.float32)
    xpos = (xstart + jnp.arange(strip, dtype=jnp.int32) + patch_offsets[1]).astype(jnp.float32)
    ypos = (jnp.arange(width, dtype=jnp.int32) + patch_offsets[2]).astype(jnp.float32)
    zcos = jnp.cos(zpos * (two_pi / 61.0))
    xcos = jnp.cos(xpos * (two_pi / 37.0))[:, None]
    ysin = jnp.sin(ypos * (two_pi / 53.0))[None, :]
    plane = jax.ShapeDtypeStruct((slab, strip, width), jnp.float32)
    flat = jax.ShapeDtypeStruct((strip, width), jnp.float32)
    stokes_q, stokes_u, slab_sums, own_total, highest, lowest = pl.pallas_call(
        field_kernel,
        out_shape=(plane, plane, plane, flat, flat, flat),
        in_specs=[smem] + [vmem] * 7,
        out_specs=(vmem,) * 6,
        compiler_params=params,
    )(zcos, potential, zlow, zhigh, xlow, xhigh, xcos, ysin)

    middle, table = series_table()
    tile_count = lax.axis_size("tile")
    chunks, chip_count = strip // 8, depth_count // 2
    half = (TERMS, 8, width)
    small = (8, 128)
    dma = pltpu.SemaphoreType.DMA
    pair = [dma((depth_count - 1,))] * 4 + [dma((tile_count - 1,))] * 2
    moments, faraday_depth, farthest = pl.pallas_call(
        functools.partial(moment_kernel, float(middle)),
        out_shape=(
            jax.ShapeDtypeStruct((2, TERMS, strip, width), jnp.float32),
            flat,
            jax.ShapeDtypeStruct(small, jnp.float32),
        ),
        in_specs=[vmem] * 6,
        out_specs=(vmem,) * 3,
        scratch_shapes=[
            pltpu.VMEM((depth_count - 1, strip, width), jnp.float32),
            pltpu.VMEM((strip, width), jnp.float32),
            pltpu.VMEM((chunks, 2) + half, jnp.float32),
            pltpu.VMEM((chunks,) + half, jnp.float32),
            pltpu.VMEM((chunks,) + half, jnp.float32),
            pltpu.VMEM((chunks, chip_count - 1) + half, jnp.float32),
            pltpu.VMEM(small, jnp.float32),
            pltpu.VMEM((depth_count - 1,) + small, jnp.float32),
            pltpu.VMEM(small, jnp.float32),
            pltpu.VMEM((tile_count - 1,) + small, jnp.float32),
        ]
        + pair
        + [dma((chunks,))] * 2
        + [dma((chunks, chip_count - 1))] * 2
        + [dma((chunks,))] * 2,
        compiler_params=pltpu.CompilerParams(
            collective_id=1, has_side_effects=True, vmem_limit_bytes=60 * 1024 * 1024
        ),
    )(stokes_q, stokes_u, slab_sums, own_total, highest, lowest)
    farthest = jnp.max(farthest)

    freq = 0.5 + 1.5 * channel_index.astype(jnp.float32) / (NCH - 1)
    lam2 = (0.2998 / freq) ** 2
    weight = 1.0 / (freq * jnp.sqrt(jnp.float32(slab * depth_count)))
    rows = NCH // depth_count

    def own(values):
        return lax.dynamic_slice_in_dim(values, depth_place * rows, rows)

    def by_series(_):
        return pl.pallas_call(
            channel_kernel,
            out_shape=jax.ShapeDtypeStruct((rows, 2, strip, width), jnp.float32),
            in_specs=[smem] * 4 + [vmem] * 2,
            out_specs=vmem,
            compiler_params=params,
        )(
            own(channel_index),
            own(lam2),
            own(weight),
            jnp.asarray(table.reshape(-1)),
            moments,
            faraday_depth,
        )

    def by_sum(_):
        totals = lax.all_gather(own_total, "depth")
        before = (jnp.arange(depth_count) < depth_place)[:, None, None]
        nearer = jnp.sum(jnp.where(before, totals, 0.0), axis=0)
        whole = pl.BlockSpec((slab, strip, width), lambda c: (0, 0, 0))
        sums = pl.pallas_call(
            direct_kernel,
            grid=(NCH,),
            out_shape=jax.ShapeDtypeStruct((NCH, 2, strip, width), jnp.float32),
            in_specs=[smem] * 2
            + [whole] * 3
            + [pl.BlockSpec((strip, width), lambda c: (0, 0))],
            out_specs=pl.BlockSpec((1, 2, strip, width), lambda c: (c, 0, 0, 0)),
            compiler_params=params,
        )(lam2, weight, stokes_q, stokes_u, slab_sums, nearer)
        return lax.psum_scatter(sums, "depth", scatter_dimension=0, tiled=True)

    pol_spectra = lax.cond(farthest <= REACH, by_series, by_sum, 0)
    return (pol_spectra, faraday_depth)


def solution(mesh):
    in_specs = (P(None, "depth", "tile", None), P(), P())
    out_specs = (P("depth", None, "tile", None), P("tile", None))
    return jax.shard_map(body, mesh=mesh, in_specs=in_specs, out_specs=out_specs, check_vma=False)
```

```python
import functools

import jax
import jax.numpy as jnp
import numpy as np
from jax import lax
from jax.experimental import pallas as pl
from jax.experimental.pallas import tpu as pltpu
from jax.sharding import PartitionSpec as P

NCH = 64


two_pi = 6.283185307179586
faraday_coef = 0.25

REACH = 24.0
TERMS = 22


def grid_lam2():
    freq = 0.5 + 1.5 * np.arange(NCH, dtype=np.float64) / (NCH - 1)
    return 2.0 * (0.2998 / freq) ** 2


def series_table():
    lam = grid_lam2()
    middle = 0.5 * (lam.max() + lam.min())
    args = (lam - middle) * REACH
    count = 4096
    theta = (np.arange(count) + 0.5) * (np.pi / count)
    orders = np.arange(TERMS)
    table = np.cos(
        orders[None, :, None] * theta - args[:, None, None] * np.sin(theta)
    ).mean(axis=-1)
    table = table * np.where(orders == 0, 1.0, 2.0)
    table = table * np.where((orders // 2) % 2 == 0, 1.0, -1.0)
    return middle, table.astype(np.float32)


def halves_fit():
    nodes = 0.25 * (np.cos((np.arange(200) + 0.5) * np.pi / 200) + 1.0) / 2.0
    r = np.sqrt(nodes)
    root = np.sqrt(2.0)
    sin_fit = np.polynomial.polynomial.polyfit(nodes, root * np.sin(np.pi * r) / r, 4)
    cos_fit = np.polynomial.polynomial.polyfit(nodes, root * np.cos(np.pi * r), 5)
    return [float(v) for v in sin_fit], [float(v) for v in cos_fit]


SIN_FIT, COS_FIT = halves_fit()


def horner(fit, square):
    total = fit[-1] * square + fit[-2]
    for value in fit[-3::-1]:
        total = total * square + value
    return total


def turn(fraction):
    square = fraction * fraction
    sine = horner(SIN_FIT, square) * fraction
    cosine = horner(COS_FIT, square)
    return 1.0 - sine * sine, sine * cosine


def turn_of_phase(phase):
    laps = jnp.round(phase * (1.0 / two_pi))
    rest = phase - laps * 6.28125
    rest = rest - laps * 0.0019340515136718750
    rest = rest - laps * (two_pi - 6.28125 - 0.0019340515136718750)
    return turn(rest * (1.0 / two_pi))


def field_kernel(zcos, pot, zlow, zhigh, xlow, xhigh, xcos, ysin, q_out, u_out, sum_out, total_out, high_out, low_out):
    slab, strip, width = sum_out.shape
    column = lax.broadcasted_iota(jnp.int32, (strip, width), 1)
    ybase = jnp.broadcast_to(1.0 + 0.3 * ysin[...], (strip, width))
    xhalf = jnp.broadcast_to(0.5 * xcos[...], (strip, width))

    def along_last(v):
        up1 = jnp.where(column < width - 1, pltpu.roll(v, width - 1, 1), 0.0)
        up2 = jnp.where(column < width - 2, pltpu.roll(v, width - 2, 1), 0.0)
        down1 = jnp.where(column >= 1, pltpu.roll(v, 1, 1), 0.0)
        down2 = jnp.where(column >= 2, pltpu.roll(v, 2, 1), 0.0)
        return (8.0 * (up1 - down1) - (up2 - down2)) * (1.0 / 12.0)

    def along_mid(component, z):
        low = xlow[component - 1, z]
        high = xhigh[component - 1, z]
        v = jnp.concatenate([low, pot[component, z], high], axis=0)
        return (8.0 * (v[3 : strip + 3] - v[1 : strip + 1]) - (v[4 : strip + 4] - v[0:strip])) * (
            1.0 / 12.0
        )

    def along_lead(component, z, edge):
        def plane(step):
            if edge is None:
                return pot[component, z + step]
            place = edge + step
            if place < 0:
                return zlow[component, place + 2]
            if place >= slab:
                return zhigh[component, place - slab]
            return pot[component, place]

        return (8.0 * (plane(1) - plane(-1)) - (plane(2) - plane(-2))) * (1.0 / 12.0)

    def one(z, state, edge=None):
        before, high, low = state
        field_x = along_last(pot[2, z]) - along_lead(1, z, edge)
        field_y = along_lead(0, z, edge) - along_mid(2, z)
        field_z = along_mid(1, z) - along_last(pot[0, z])
        density = ybase + zcos[z] * xhalf
        q_out[z] = density * (field_y * field_y - field_x * field_x)
        u_out[z] = -2.0 * density * field_x * field_y
        now = before + density * field_z
        sum_out[z] = now
        return now, jnp.maximum(high, now), jnp.minimum(low, now)

    zero = jnp.zeros((strip, width), jnp.float32)
    state = (zero, zero, zero)
    for z in (0, 1):
        state = one(z, state, z)
    state = lax.fori_loop(2, slab - 2, one, state)
    for z in (slab - 2, slab - 1):
        state = one(z, state, z)
    total_out[...] = faraday_coef * state[0]
    high_out[...] = faraday_coef * state[1]
    low_out[...] = faraday_coef * state[2]


def halo_kernel(zup, zdown, xup, xdown, zlow, zhigh, xlow, xhigh, send, recv):
    barrier = pltpu.get_barrier_semaphore()
    plan = []
    for order, (axis, up, down, low, high) in enumerate(
        (("depth", zup, zdown, zlow, zhigh), ("tile", xup, xdown, xlow, xhigh))
    ):
        place = lax.axis_index(axis)
        last = lax.axis_size(axis) - 1
        above = pltpu.make_async_remote_copy(
            src_ref=up, dst_ref=low, send_sem=send.at[2 * order], recv_sem=recv.at[2 * order],
            device_id={axis: place + 1}, device_id_type=pl.DeviceIdType.MESH,
        )
        below = pltpu.make_async_remote_copy(
            src_ref=down, dst_ref=high, send_sem=send.at[2 * order + 1],
            recv_sem=recv.at[2 * order + 1],
            device_id={axis: place - 1}, device_id_type=pl.DeviceIdType.MESH,
        )
        plan.append((axis, place, last, above, below, low, high))

    def signal(axis, index):
        pl.semaphore_signal(
            barrier, inc=1, device_id={axis: index}, device_id_type=pl.DeviceIdType.MESH
        )

    for axis, place, last, above, below, low, high in plan:
        pl.when(place > 0)(functools.partial(signal, axis, place - 1))
        pl.when(place < last)(functools.partial(signal, axis, place + 1))
    count = 0
    for axis, place, last, above, below, low, high in plan:
        count = count + (place + last - 1) // last + (2 * last - place - 1) // last
    pl.semaphore_wait(barrier, count)
    for axis, place, last, above, below, low, high in reversed(plan):
        pl.when(place < last)(above.start)
        pl.when(place > 0)(below.start)
    for axis, place, last, above, below, low, high in plan:

        @pl.when(place == 0)
        def _():
            low[...] = jnp.zeros_like(low)

        @pl.when(place == last)
        def _():
            high[...] = jnp.zeros_like(high)

    for axis, place, last, above, below, low, high in plan:

        @pl.when(place < last)
        def _():
            above.wait_send()
            below.wait_recv()

        @pl.when(place > 0)
        def _():
            below.wait_send()
            above.wait_recv()


def moment_kernel(
    middle, q_ref, u_ref, sum_ref, total_ref, high_ref, low_ref,
    out, depth_out, far_out, start_ref,
    others, own, near, part, across, far, far_depth, far_mid, far_tile,
    carry_send, carry_recv, far_send, far_recv, tile_send, tile_recv,
    near_send, near_recv, cross_send, cross_recv, back_send, back_recv,
):
    slab, strip, width = sum_ref.shape
    group = 8 if slab % 8 == 0 else 1
    chunks = strip // 8
    depth_count, tile_count = lax.axis_size("depth"), lax.axis_size("tile")
    depth_place, tile_place = lax.axis_index("depth"), lax.axis_index("tile")
    core = lax.rem(depth_place, 2)
    chip_count = depth_count // 2
    chip = depth_place // 2
    partner = depth_place + 1 - 2 * core

    def copy(src, dst, send, recv, axis, index):
        return pltpu.make_async_remote_copy(
            src_ref=src, dst_ref=dst, send_sem=send, recv_sem=recv,
            device_id={axis: index}, device_id_type=pl.DeviceIdType.MESH,
        )

    def depth_peer(k):
        return lax.rem(depth_place + k, depth_count)

    def tile_peer(k):
        return lax.rem(tile_place + k, tile_count)

    barrier = pltpu.get_barrier_semaphore()
    for k in range(1, depth_count):
        pl.semaphore_signal(
            barrier, inc=1, device_id={"depth": depth_peer(k)},
            device_id_type=pl.DeviceIdType.MESH,
        )
    for k in range(1, tile_count):
        pl.semaphore_signal(
            barrier, inc=1, device_id={"tile": tile_peer(k)},
            device_id_type=pl.DeviceIdType.MESH,
        )
    pl.semaphore_wait(barrier, depth_count + tile_count - 2)

    carries = [
        copy(total_ref, others.at[k - 1], carry_send.at[k - 1], carry_recv.at[k - 1],
             "depth", depth_peer(k))
        for k in range(1, depth_count)
    ]
    for item in carries:
        item.start()
    for item in carries:
        item.wait()
    nearer = jnp.zeros((strip, width), jnp.float32)
    whole = total_ref[...]
    for k in range(1, depth_count):
        part_k = others[k - 1]
        whole = whole + part_k
        nearer = nearer + jnp.where(depth_place >= k, part_k, 0.0)
    depth_out[...] = whole
    start = nearer - 0.5 * whole
    start_ref[...] = start
    reach = jnp.maximum(jnp.abs(high_ref[...] + start), jnp.abs(low_ref[...] + start))
    reach = functools.reduce(
        jnp.maximum, [reach[:, k * 128 : (k + 1) * 128] for k in range(width // 128)]
    )
    far[...] = functools.reduce(jnp.maximum, [reach[k * 8 : k * 8 + 8] for k in range(chunks)])
    fars = [
        copy(far, far_depth.at[k - 1], far_send.at[k - 1], far_recv.at[k - 1],
             "depth", depth_peer(k))
        for k in range(1, depth_count)
    ]
    for item in fars:
        item.start()

    def tile(row, col, g):
        rows = pl.ds(pl.multiple_of(row, 8), 8)
        cols = pl.ds(pl.multiple_of(col, 128), 128)
        place = (rows, cols)
        start = start_ref[place]
        for half in range(2):
            for j in range(TERMS):
                own[g, half, j, :, cols] = jnp.zeros((8, 128), jnp.float32)

        def block(step, carry):
            q_prev, q_now, u_prev, u_now, twice = [], [], [], [], []
            for k in range(group):
                z = step * group + k
                shift = faraday_coef * sum_ref[(z,) + place] + start
                laps = shift * (middle / two_pi)
                cosine, sine = turn(laps - jnp.round(laps))
                q = q_ref[(z,) + place]
                u = u_ref[(z,) + place]
                x = shift * (1.0 / REACH)
                q_prev.append(q * cosine - u * sine)
                u_prev.append(q * sine + u * cosine)
                twice.append(x + x)
                q_now.append(x * q_prev[-1])
                u_now.append(x * u_prev[-1])
            own[g, 0, 0, :, cols] += functools.reduce(jnp.add, q_prev)
            own[g, 1, 0, :, cols] += functools.reduce(jnp.add, u_prev)
            for j in range(1, TERMS):
                own[g, 0, j, :, cols] += functools.reduce(jnp.add, q_now)
                own[g, 1, j, :, cols] += functools.reduce(jnp.add, u_now)
                if j < TERMS - 1:
                    for k in range(group):
                        q_prev[k], q_now[k] = q_now[k], twice[k] * q_now[k] - q_prev[k]
                        u_prev[k], u_now[k] = u_now[k], twice[k] * u_now[k] - u_prev[k]
            return carry

        lax.fori_loop(0, slab // group, block, 0)

    def near_copy(g):
        return copy(own.at[g, 1 - core], near.at[g], near_send.at[g], near_recv.at[g],
                    "depth", partner)

    def cross_copies(g):
        return [
            copy(part.at[g], across.at[g, k - 1], cross_send.at[g, k - 1],
                 cross_recv.at[g, k - 1], "depth", 2 * lax.rem(chip + k, chip_count) + core)
            for k in range(1, chip_count)
        ]

    def back_copy(g):
        piece = out.at[core, :, pl.ds(pl.multiple_of(g * 8, 8), 8)]
        return copy(piece, piece, back_send.at[g], back_recv.at[g], "depth", partner)

    def compute(g):
        lax.fori_loop(
            0, width // 128, lambda c, carry: (tile(g * 8, c * 128, g), carry)[1], 0
        )
        near_copy(g).start()

    def sum_chip(g):
        near_copy(g).wait()
        part[g] = own[g, core] + near[g]
        for item in cross_copies(g):
            item.start()

    def sum_all(g):
        total = part[g]
        for k, item in enumerate(cross_copies(g)):
            item.wait()
            total = total + across[g, k]
        out[core, :, pl.ds(pl.multiple_of(g * 8, 8), 8)] = total
        back_copy(g).start()

    tiles_far = [
        copy(far_mid, far_tile.at[k - 1], tile_send.at[k - 1], tile_recv.at[k - 1],
             "tile", tile_peer(k))
        for k in range(1, tile_count)
    ]

    def lap(g, carry):
        pl.when(g < chunks)(lambda: compute(g))

        @pl.when(g == 0)
        def _():
            reach = far[...]
            for k, item in enumerate(fars):
                item.wait()
                reach = jnp.maximum(reach, far_depth[k])
            far_mid[...] = reach
            for item in tiles_far:
                item.start()

        pl.when(g < chunks)(lambda: sum_chip(g))
        pl.when(g >= 1)(lambda: sum_all(g - 1))
        return carry

    lax.fori_loop(0, chunks + 1, lap, 0)
    reach = far_mid[...]
    for k, item in enumerate(tiles_far):
        item.wait()
        reach = jnp.maximum(reach, far_tile[k])
    far_out[...] = reach
    for g in range(chunks):
        back_copy(g).wait()


def channel_kernel(index, lam, weight, table, moments, depth_ref, out):
    rows, _, strip, width = out.shape
    first_row = lax.axis_index("depth") * rows

    def band(step, carry):
        place = pl.ds(pl.multiple_of(step * 8, 8), 8)
        half = 0.5 * depth_ref[place]

        def one(row, carry):
            base = index[first_row + row] * TERMS
            real_part = table[base] * moments[0, 0, place]
            imag_part = table[base] * moments[1, 0, place]
            for j in range(1, TERMS):
                factor = table[base + j]
                first = factor * moments[0, j, place]
                second = factor * moments[1, j, place]
                if j % 2 == 0:
                    real_part = real_part + first
                    imag_part = imag_part + second
                else:
                    real_part = real_part - second
                    imag_part = imag_part + first
            cosine, sine = turn_of_phase(2.0 * lam[first_row + row] * half)
            out[row, 0, place] = (real_part * cosine - imag_part * sine) * weight[first_row + row]
            out[row, 1, place] = (real_part * sine + imag_part * cosine) * weight[first_row + row]
            return carry

        return lax.fori_loop(0, rows, one, carry)

    lax.fori_loop(0, strip // 8, band, 0)


def direct_kernel(lam, weight, q_ref, u_ref, sum_ref, nearer_ref, out):
    slab, strip, width = sum_ref.shape
    twice = 2.0 * lam[pl.program_id(0)]
    scale = weight[pl.program_id(0)]

    def band(step, carry):
        place = pl.ds(pl.multiple_of(step * 8, 8), 8)
        nearer = nearer_ref[place]

        def one(z, sums):
            cosine, sine = turn_of_phase(twice * (faraday_coef * sum_ref[z, place] + nearer))
            q = q_ref[z, place]
            u = u_ref[z, place]
            return sums[0] + (q * cosine - u * sine), sums[1] + (q * sine + u * cosine)

        zero = jnp.zeros((8, width), jnp.float32)
        real_part, imag_part = lax.fori_loop(0, slab, one, (zero, zero))
        out[0, 0, place] = real_part * scale
        out[0, 1, place] = imag_part * scale
        return carry

    lax.fori_loop(0, strip // 8, band, 0)


vmem = pl.BlockSpec(memory_space=pltpu.VMEM)
smem = pl.BlockSpec(memory_space=pltpu.SMEM)
params = pltpu.CompilerParams(vmem_limit_bytes=60 * 1024 * 1024)


def body(potential, channel_index, patch_offsets):
    depth_count = lax.axis_size("depth")
    depth_place = lax.axis_index("depth")
    slab, strip, width = (potential.shape[1], potential.shape[2], potential.shape[3])
    shapes = [(2, 2, strip, width)] * 2 + [(2, slab, 2, width)] * 2
    zlow, zhigh, xlow, xhigh = pl.pallas_call(
        halo_kernel,
        out_shape=tuple(jax.ShapeDtypeStruct(shape, jnp.float32) for shape in shapes),
        in_specs=[vmem] * 4,
        out_specs=(vmem,) * 4,
        scratch_shapes=[pltpu.SemaphoreType.DMA((4,)), pltpu.SemaphoreType.DMA((4,))],
        compiler_params=pltpu.CompilerParams(collective_id=0, has_side_effects=True),
    )(
        potential[0:2, slab - 2 :],
        potential[0:2, :2],
        potential[1:3, :, strip - 2 :],
        potential[1:3, :, :2],
    )
    zstart = depth_place * slab
    xstart = lax.axis_index("tile") * strip
    zpos = (zstart + jnp.arange(slab, dtype=jnp.int32) + patch_offsets[0]).astype(jnp.float32)
    xpos = (xstart + jnp.arange(strip, dtype=jnp.int32) + patch_offsets[1]).astype(jnp.float32)
    ypos = (jnp.arange(width, dtype=jnp.int32) + patch_offsets[2]).astype(jnp.float32)
    zcos = jnp.cos(zpos * (two_pi / 61.0))
    xcos = jnp.cos(xpos * (two_pi / 37.0))[:, None]
    ysin = jnp.sin(ypos * (two_pi / 53.0))[None, :]
    plane = jax.ShapeDtypeStruct((slab, strip, width), jnp.float32)
    flat = jax.ShapeDtypeStruct((strip, width), jnp.float32)
    stokes_q, stokes_u, slab_sums, own_total, highest, lowest = pl.pallas_call(
        field_kernel,
        out_shape=(plane, plane, plane, flat, flat, flat),
        in_specs=[smem] + [vmem] * 7,
        out_specs=(vmem,) * 6,
        compiler_params=params,
    )(zcos, potential, zlow, zhigh, xlow, xhigh, xcos, ysin)

    middle, table = series_table()
    tile_count = lax.axis_size("tile")
    chunks, chip_count = strip // 8, depth_count // 2
    half = (TERMS, 8, width)
    small = (8, 128)
    dma = pltpu.SemaphoreType.DMA
    pair = [dma((depth_count - 1,))] * 4 + [dma((tile_count - 1,))] * 2
    moments, faraday_depth, farthest, start = pl.pallas_call(
        functools.partial(moment_kernel, float(middle)),
        out_shape=(
            jax.ShapeDtypeStruct((2, TERMS, strip, width), jnp.float32),
            flat,
            jax.ShapeDtypeStruct(small, jnp.float32),
            flat,
        ),
        in_specs=[vmem] * 6,
        out_specs=(vmem,) * 4,
        scratch_shapes=[
            pltpu.VMEM((depth_count - 1, strip, width), jnp.float32),
            pltpu.VMEM((chunks, 2) + half, jnp.float32),
            pltpu.VMEM((chunks,) + half, jnp.float32),
            pltpu.VMEM((chunks,) + half, jnp.float32),
            pltpu.VMEM((chunks, chip_count - 1) + half, jnp.float32),
            pltpu.VMEM(small, jnp.float32),
            pltpu.VMEM((depth_count - 1,) + small, jnp.float32),
            pltpu.VMEM(small, jnp.float32),
            pltpu.VMEM((tile_count - 1,) + small, jnp.float32),
        ]
        + pair
        + [dma((chunks,))] * 2
        + [dma((chunks, chip_count - 1))] * 2
        + [dma((chunks,))] * 2,
        compiler_params=pltpu.CompilerParams(
            collective_id=1, has_side_effects=True, vmem_limit_bytes=60 * 1024 * 1024
        ),
    )(stokes_q, stokes_u, slab_sums, own_total, highest, lowest)
    farthest = jnp.max(farthest)

    freq = 0.5 + 1.5 * channel_index.astype(jnp.float32) / (NCH - 1)
    lam2 = (0.2998 / freq) ** 2
    weight = 1.0 / (freq * jnp.sqrt(jnp.float32(slab * depth_count)))
    rows = NCH // depth_count

    def by_series(_):
        return pl.pallas_call(
            channel_kernel,
            out_shape=jax.ShapeDtypeStruct((rows, 2, strip, width), jnp.float32),
            in_specs=[smem] * 4 + [vmem] * 2,
            out_specs=vmem,
            compiler_params=params,
        )(
            channel_index,
            lam2,
            weight,
            jnp.asarray(table.reshape(-1)),
            moments,
            faraday_depth,
        )

    def by_sum(_):
        nearer = start + 0.5 * faraday_depth
        whole = pl.BlockSpec((slab, strip, width), lambda c: (0, 0, 0))
        sums = pl.pallas_call(
            direct_kernel,
            grid=(NCH,),
            out_shape=jax.ShapeDtypeStruct((NCH, 2, strip, width), jnp.float32),
            in_specs=[smem] * 2
            + [whole] * 3
            + [pl.BlockSpec((strip, width), lambda c: (0, 0))],
            out_specs=pl.BlockSpec((1, 2, strip, width), lambda c: (c, 0, 0, 0)),
            compiler_params=params,
        )(lam2, weight, stokes_q, stokes_u, slab_sums, nearer)
        sums = sums.reshape(depth_count, rows, 2, strip, width)
        return jnp.sum(lax.all_to_all(sums, "depth", 0, 0), axis=0)

    pol_spectra = lax.cond(farthest <= REACH, by_series, by_sum, 0)
    return (pol_spectra, faraday_depth)


def solution(mesh):
    in_specs = (P(None, "depth", "tile", None), P(), P())
    out_specs = (P("depth", None, "tile", None), P("tile", None))
    return jax.shard_map(body, mesh=mesh, in_specs=in_specs, out_specs=out_specs, check_vma=False)
```

```python
import functools

import jax
import jax.numpy as jnp
import numpy as np
from jax import lax
from jax.experimental import pallas as pl
from jax.experimental.pallas import tpu as pltpu
from jax.sharding import PartitionSpec as P

NCH = 64


two_pi = 6.283185307179586
faraday_coef = 0.25

REACH = 24.0
TERMS = 22


def grid_lam2():
    freq = 0.5 + 1.5 * np.arange(NCH, dtype=np.float64) / (NCH - 1)
    return 2.0 * (0.2998 / freq) ** 2


def series_table():
    lam = grid_lam2()
    middle = 0.5 * (lam.max() + lam.min())
    args = (lam - middle) * REACH
    count = 4096
    theta = (np.arange(count) + 0.5) * (np.pi / count)
    orders = np.arange(TERMS)
    table = np.cos(
        orders[None, :, None] * theta - args[:, None, None] * np.sin(theta)
    ).mean(axis=-1)
    table = table * np.where(orders == 0, 1.0, 2.0)
    table = table * np.where((orders // 2) % 2 == 0, 1.0, -1.0)
    return middle, table.astype(np.float32)


def halves_fit():
    nodes = 0.25 * (np.cos((np.arange(200) + 0.5) * np.pi / 200) + 1.0) / 2.0
    r = np.sqrt(nodes)
    root = np.sqrt(2.0)
    sin_fit = np.polynomial.polynomial.polyfit(nodes, root * np.sin(np.pi * r) / r, 4)
    cos_fit = np.polynomial.polynomial.polyfit(nodes, root * np.cos(np.pi * r), 5)
    return [float(v) for v in sin_fit], [float(v) for v in cos_fit]


SIN_FIT, COS_FIT = halves_fit()


def horner(fit, square):
    total = fit[-1] * square + fit[-2]
    for value in fit[-3::-1]:
        total = total * square + value
    return total


def turn(fraction):
    square = fraction * fraction
    sine = horner(SIN_FIT, square) * fraction
    cosine = horner(COS_FIT, square)
    return 1.0 - sine * sine, sine * cosine


def turn_of_phase(phase):
    laps = jnp.round(phase * (1.0 / two_pi))
    rest = phase - laps * 6.28125
    rest = rest - laps * 0.0019340515136718750
    rest = rest - laps * (two_pi - 6.28125 - 0.0019340515136718750)
    return turn(rest * (1.0 / two_pi))


def field_kernel(
    zcos, pot, zup, zdown, xup, xdown, xcos, ysin,
    q_out, u_out, sum_out, total_out, high_out, low_out,
    zlow, zhigh, xlow, xhigh, send, recv,
):
    slab, strip, width = sum_out.shape
    bands = strip // 8
    barrier = pltpu.get_barrier_semaphore()
    plan = []
    for order, (axis, up, down, low, high) in enumerate(
        (("depth", zup, zdown, zlow, zhigh), ("tile", xup, xdown, xlow, xhigh))
    ):
        place = lax.axis_index(axis)
        last = lax.axis_size(axis) - 1
        above = pltpu.make_async_remote_copy(
            src_ref=up, dst_ref=low, send_sem=send.at[2 * order], recv_sem=recv.at[2 * order],
            device_id={axis: place + 1}, device_id_type=pl.DeviceIdType.MESH,
        )
        below = pltpu.make_async_remote_copy(
            src_ref=down, dst_ref=high, send_sem=send.at[2 * order + 1],
            recv_sem=recv.at[2 * order + 1],
            device_id={axis: place - 1}, device_id_type=pl.DeviceIdType.MESH,
        )
        plan.append((axis, place, last, above, below, low, high))

    def signal(axis, index):
        pl.semaphore_signal(
            barrier, inc=1, device_id={axis: index}, device_id_type=pl.DeviceIdType.MESH
        )

    count = 0
    for axis, place, last, above, below, low, high in plan:
        pl.when(place > 0)(functools.partial(signal, axis, place - 1))
        pl.when(place < last)(functools.partial(signal, axis, place + 1))
        count = count + (place + last - 1) // last + (2 * last - place - 1) // last
    pl.semaphore_wait(barrier, count)
    for axis, place, last, above, below, low, high in plan:
        pl.when(place < last)(above.start)
        pl.when(place > 0)(below.start)
    for axis, place, last, above, below, low, high in plan:

        @pl.when(place == 0)
        def _():
            low[...] = jnp.zeros_like(low)

        @pl.when(place == last)
        def _():
            high[...] = jnp.zeros_like(high)

    def arrive(axis, place, last, above, below, low, high):
        @pl.when(place < last)
        def _():
            above.wait_send()
            below.wait_recv()

        @pl.when(place > 0)
        def _():
            below.wait_send()
            above.wait_recv()

    column = lax.broadcasted_iota(jnp.int32, (8, width), 1)

    def along_last(v):
        up1 = jnp.where(column < width - 1, pltpu.roll(v, width - 1, 1), 0.0)
        up2 = jnp.where(column < width - 2, pltpu.roll(v, width - 2, 1), 0.0)
        down1 = jnp.where(column >= 1, pltpu.roll(v, 1, 1), 0.0)
        down2 = jnp.where(column >= 2, pltpu.roll(v, 2, 1), 0.0)
        return (8.0 * (up1 - down1) - (up2 - down2)) * (1.0 / 12.0)

    def one_band(band):
        rows = slice(8 * band, 8 * band + 8)
        ybase = jnp.broadcast_to(1.0 + 0.3 * ysin[...], (8, width))
        xhalf = jnp.broadcast_to(0.5 * xcos[rows], (8, width))

        def along_mid(component, z):
            if band == 0:
                v = jnp.concatenate([xlow[component - 1, z], pot[component, z, 0:16]], axis=0)
                at = 0
            elif band == bands - 1:
                v = jnp.concatenate(
                    [pot[component, z, strip - 16 : strip], xhigh[component - 1, z]], axis=0
                )
                at = 6
            else:
                v = pot[component, z, 8 * band - 8 : 8 * band + 16]
                at = 6
            return (
                8.0 * (v[at + 3 : at + 11] - v[at + 1 : at + 9])
                - (v[at + 4 : at + 12] - v[at : at + 8])
            ) * (1.0 / 12.0)

        def along_lead(component, z, edge):
            def plane(step):
                if edge is None:
                    return pot[component, z + step, rows]
                place = edge + step
                if place < 0:
                    return zlow[component, place + 2, rows]
                if place >= slab:
                    return zhigh[component, place - slab, rows]
                return pot[component, place, rows]

            return (8.0 * (plane(1) - plane(-1)) - (plane(2) - plane(-2))) * (1.0 / 12.0)

        def one(z, state, edge=None):
            before, high, low = state
            field_x = along_last(pot[2, z, rows]) - along_lead(1, z, edge)
            field_y = along_lead(0, z, edge) - along_mid(2, z)
            field_z = along_mid(1, z) - along_last(pot[0, z, rows])
            density = ybase + zcos[z] * xhalf
            q_out[z, rows] = density * (field_y * field_y - field_x * field_x)
            u_out[z, rows] = -2.0 * density * field_x * field_y
            now = before + density * field_z
            sum_out[z, rows] = now
            return now, jnp.maximum(high, now), jnp.minimum(low, now)

        zero = jnp.zeros((8, width), jnp.float32)
        state = (zero, zero, zero)
        for z in (0, 1):
            state = one(z, state, z)
        state = lax.fori_loop(2, slab - 2, one, state)
        for z in (slab - 2, slab - 1):
            state = one(z, state, z)
        total_out[rows] = faraday_coef * state[0]
        high_out[rows] = faraday_coef * state[1]
        low_out[rows] = faraday_coef * state[2]

    arrive(*plan[0])
    for band in range(1, bands - 1):
        one_band(band)
    arrive(*plan[1])
    for band in (0, bands - 1):
        one_band(band)


def moment_kernel(
    middle, q_ref, u_ref, sum_ref, total_ref, high_ref, low_ref,
    out, depth_out, far_out, start_ref,
    others, own, near, part, across, far, far_depth, far_mid, far_tile,
    carry_send, carry_recv, far_send, far_recv, tile_send, tile_recv,
    near_send, near_recv, cross_send, cross_recv, back_send, back_recv,
):
    slab, strip, width = sum_ref.shape
    group = 8 if slab % 8 == 0 else 1
    chunks = strip // 8
    depth_count, tile_count = lax.axis_size("depth"), lax.axis_size("tile")
    depth_place, tile_place = lax.axis_index("depth"), lax.axis_index("tile")
    core = lax.rem(depth_place, 2)
    chip_count = depth_count // 2
    chip = depth_place // 2
    partner = depth_place + 1 - 2 * core

    def copy(src, dst, send, recv, axis, index):
        return pltpu.make_async_remote_copy(
            src_ref=src, dst_ref=dst, send_sem=send, recv_sem=recv,
            device_id={axis: index}, device_id_type=pl.DeviceIdType.MESH,
        )

    def depth_peer(k):
        return lax.rem(depth_place + k, depth_count)

    def tile_peer(k):
        return lax.rem(tile_place + k, tile_count)

    barrier = pltpu.get_barrier_semaphore()
    for k in range(1, depth_count):
        pl.semaphore_signal(
            barrier, inc=1, device_id={"depth": depth_peer(k)},
            device_id_type=pl.DeviceIdType.MESH,
        )
    for k in range(1, tile_count):
        pl.semaphore_signal(
            barrier, inc=1, device_id={"tile": tile_peer(k)},
            device_id_type=pl.DeviceIdType.MESH,
        )
    pl.semaphore_wait(barrier, depth_count + tile_count - 2)

    carries = [
        copy(total_ref, others.at[k - 1], carry_send.at[k - 1], carry_recv.at[k - 1],
             "depth", depth_peer(k))
        for k in range(1, depth_count)
    ]
    for item in carries:
        item.start()
    for item in carries:
        item.wait()
    nearer = jnp.zeros((strip, width), jnp.float32)
    whole = total_ref[...]
    for k in range(1, depth_count):
        part_k = others[k - 1]
        whole = whole + part_k
        nearer = nearer + jnp.where(depth_place >= k, part_k, 0.0)
    depth_out[...] = whole
    start = nearer - 0.5 * whole
    start_ref[...] = start
    reach = jnp.maximum(jnp.abs(high_ref[...] + start), jnp.abs(low_ref[...] + start))
    reach = functools.reduce(
        jnp.maximum, [reach[:, k * 128 : (k + 1) * 128] for k in range(width // 128)]
    )
    far[...] = functools.reduce(jnp.maximum, [reach[k * 8 : k * 8 + 8] for k in range(chunks)])
    fars = [
        copy(far, far_depth.at[k - 1], far_send.at[k - 1], far_recv.at[k - 1],
             "depth", depth_peer(k))
        for k in range(1, depth_count)
    ]
    for item in fars:
        item.start()

    def tile(row, col, g):
        rows = pl.ds(pl.multiple_of(row, 8), 8)
        cols = pl.ds(pl.multiple_of(col, 128), 128)
        place = (rows, cols)
        start = start_ref[place]
        for half in range(2):
            for j in range(TERMS):
                own[g, half, j, :, cols] = jnp.zeros((8, 128), jnp.float32)

        def block(step, carry):
            q_prev, q_now, u_prev, u_now, twice = [], [], [], [], []
            for k in range(group):
                z = step * group + k
                shift = faraday_coef * sum_ref[(z,) + place] + start
                laps = shift * (middle / two_pi)
                cosine, sine = turn(laps - jnp.round(laps))
                q = q_ref[(z,) + place]
                u = u_ref[(z,) + place]
                x = shift * (1.0 / REACH)
                q_prev.append(q * cosine - u * sine)
                u_prev.append(q * sine + u * cosine)
                twice.append(x + x)
                q_now.append(x * q_prev[-1])
                u_now.append(x * u_prev[-1])
            own[g, 0, 0, :, cols] += functools.reduce(jnp.add, q_prev)
            own[g, 1, 0, :, cols] += functools.reduce(jnp.add, u_prev)
            for j in range(1, TERMS):
                own[g, 0, j, :, cols] += functools.reduce(jnp.add, q_now)
                own[g, 1, j, :, cols] += functools.reduce(jnp.add, u_now)
                if j < TERMS - 1:
                    for k in range(group):
                        q_prev[k], q_now[k] = q_now[k], twice[k] * q_now[k] - q_prev[k]
                        u_prev[k], u_now[k] = u_now[k], twice[k] * u_now[k] - u_prev[k]
            return carry

        lax.fori_loop(0, slab // group, block, 0)

    def near_copy(g):
        return copy(own.at[g, 1 - core], near.at[g], near_send.at[g], near_recv.at[g],
                    "depth", partner)

    def cross_copies(g):
        return [
            copy(part.at[g], across.at[g, k - 1], cross_send.at[g, k - 1],
                 cross_recv.at[g, k - 1], "depth", 2 * lax.rem(chip + k, chip_count) + core)
            for k in range(1, chip_count)
        ]

    def back_copy(g):
        piece = out.at[core, :, pl.ds(pl.multiple_of(g * 8, 8), 8)]
        return copy(piece, piece, back_send.at[g], back_recv.at[g], "depth", partner)

    def compute(g):
        lax.fori_loop(
            0, width // 128, lambda c, carry: (tile(g * 8, c * 128, g), carry)[1], 0
        )
        near_copy(g).start()

    def sum_chip(g):
        near_copy(g).wait()
        part[g] = own[g, core] + near[g]
        for item in cross_copies(g):
            item.start()

    def sum_all(g):
        total = part[g]
        for k, item in enumerate(cross_copies(g)):
            item.wait()
            total = total + across[g, k]
        out[core, :, pl.ds(pl.multiple_of(g * 8, 8), 8)] = total
        back_copy(g).start()

    tiles_far = [
        copy(far_mid, far_tile.at[k - 1], tile_send.at[k - 1], tile_recv.at[k - 1],
             "tile", tile_peer(k))
        for k in range(1, tile_count)
    ]

    def lap(g, carry):
        pl.when(g < chunks)(lambda: compute(g))

        @pl.when(g == 0)
        def _():
            reach = far[...]
            for k, item in enumerate(fars):
                item.wait()
                reach = jnp.maximum(reach, far_depth[k])
            far_mid[...] = reach
            for item in tiles_far:
                item.start()

        pl.when(g < chunks)(lambda: sum_chip(g))
        pl.when(g >= 1)(lambda: sum_all(g - 1))
        return carry

    lax.fori_loop(0, chunks + 1, lap, 0)
    reach = far_mid[...]
    for k, item in enumerate(tiles_far):
        item.wait()
        reach = jnp.maximum(reach, far_tile[k])
    far_out[...] = reach
    for g in range(chunks):
        back_copy(g).wait()


def channel_kernel(index, lam, weight, table, moments, depth_ref, out):
    rows, _, strip, width = out.shape
    first_row = lax.axis_index("depth") * rows

    def band(step, carry):
        place = pl.ds(pl.multiple_of(step * 8, 8), 8)
        half = 0.5 * depth_ref[place]

        def one(row, carry):
            base = index[first_row + row] * TERMS
            real_part = table[base] * moments[0, 0, place]
            imag_part = table[base] * moments[1, 0, place]
            for j in range(1, TERMS):
                factor = table[base + j]
                first = factor * moments[0, j, place]
                second = factor * moments[1, j, place]
                if j % 2 == 0:
                    real_part = real_part + first
                    imag_part = imag_part + second
                else:
                    real_part = real_part - second
                    imag_part = imag_part + first
            cosine, sine = turn_of_phase(2.0 * lam[first_row + row] * half)
            out[row, 0, place] = (real_part * cosine - imag_part * sine) * weight[first_row + row]
            out[row, 1, place] = (real_part * sine + imag_part * cosine) * weight[first_row + row]
            return carry

        return lax.fori_loop(0, rows, one, carry)

    lax.fori_loop(0, strip // 8, band, 0)


def direct_kernel(lam, weight, q_ref, u_ref, sum_ref, nearer_ref, out):
    slab, strip, width = sum_ref.shape
    twice = 2.0 * lam[pl.program_id(0)]
    scale = weight[pl.program_id(0)]

    def band(step, carry):
        place = pl.ds(pl.multiple_of(step * 8, 8), 8)
        nearer = nearer_ref[place]

        def one(z, sums):
            cosine, sine = turn_of_phase(twice * (faraday_coef * sum_ref[z, place] + nearer))
            q = q_ref[z, place]
            u = u_ref[z, place]
            return sums[0] + (q * cosine - u * sine), sums[1] + (q * sine + u * cosine)

        zero = jnp.zeros((8, width), jnp.float32)
        real_part, imag_part = lax.fori_loop(0, slab, one, (zero, zero))
        out[0, 0, place] = real_part * scale
        out[0, 1, place] = imag_part * scale
        return carry

    lax.fori_loop(0, strip // 8, band, 0)


vmem = pl.BlockSpec(memory_space=pltpu.VMEM)
smem = pl.BlockSpec(memory_space=pltpu.SMEM)
params = pltpu.CompilerParams(vmem_limit_bytes=60 * 1024 * 1024)


def body(potential, channel_index, patch_offsets):
    depth_count = lax.axis_size("depth")
    depth_place = lax.axis_index("depth")
    slab, strip, width = (potential.shape[1], potential.shape[2], potential.shape[3])
    shapes = [(2, 2, strip, width)] * 2 + [(2, slab, 2, width)] * 2
    zstart = depth_place * slab
    xstart = lax.axis_index("tile") * strip
    zpos = (zstart + jnp.arange(slab, dtype=jnp.int32) + patch_offsets[0]).astype(jnp.float32)
    xpos = (xstart + jnp.arange(strip, dtype=jnp.int32) + patch_offsets[1]).astype(jnp.float32)
    ypos = (jnp.arange(width, dtype=jnp.int32) + patch_offsets[2]).astype(jnp.float32)
    zcos = jnp.cos(zpos * (two_pi / 61.0))
    xcos = jnp.cos(xpos * (two_pi / 37.0))[:, None]
    ysin = jnp.sin(ypos * (two_pi / 53.0))[None, :]
    plane = jax.ShapeDtypeStruct((slab, strip, width), jnp.float32)
    flat = jax.ShapeDtypeStruct((strip, width), jnp.float32)
    stokes_q, stokes_u, slab_sums, own_total, highest, lowest = pl.pallas_call(
        field_kernel,
        out_shape=(plane, plane, plane, flat, flat, flat),
        in_specs=[smem] + [vmem] * 7,
        out_specs=(vmem,) * 6,
        scratch_shapes=[pltpu.VMEM(shape, jnp.float32) for shape in shapes]
        + [pltpu.SemaphoreType.DMA((4,))] * 2,
        compiler_params=pltpu.CompilerParams(
            collective_id=0, has_side_effects=True, vmem_limit_bytes=60 * 1024 * 1024
        ),
    )(
        zcos,
        potential,
        potential[0:2, slab - 2 :],
        potential[0:2, :2],
        potential[1:3, :, strip - 2 :],
        potential[1:3, :, :2],
        xcos,
        ysin,
    )

    middle, table = series_table()
    tile_count = lax.axis_size("tile")
    chunks, chip_count = strip // 8, depth_count // 2
    half = (TERMS, 8, width)
    small = (8, 128)
    dma = pltpu.SemaphoreType.DMA
    pair = [dma((depth_count - 1,))] * 4 + [dma((tile_count - 1,))] * 2
    moments, faraday_depth, farthest, start = pl.pallas_call(
        functools.partial(moment_kernel, float(middle)),
        out_shape=(
            jax.ShapeDtypeStruct((2, TERMS, strip, width), jnp.float32),
            flat,
            jax.ShapeDtypeStruct(small, jnp.float32),
            flat,
        ),
        in_specs=[vmem] * 6,
        out_specs=(vmem,) * 4,
        scratch_shapes=[
            pltpu.VMEM((depth_count - 1, strip, width), jnp.float32),
            pltpu.VMEM((chunks, 2) + half, jnp.float32),
            pltpu.VMEM((chunks,) + half, jnp.float32),
            pltpu.VMEM((chunks,) + half, jnp.float32),
            pltpu.VMEM((chunks, chip_count - 1) + half, jnp.float32),
            pltpu.VMEM(small, jnp.float32),
            pltpu.VMEM((depth_count - 1,) + small, jnp.float32),
            pltpu.VMEM(small, jnp.float32),
            pltpu.VMEM((tile_count - 1,) + small, jnp.float32),
        ]
        + pair
        + [dma((chunks,))] * 2
        + [dma((chunks, chip_count - 1))] * 2
        + [dma((chunks,))] * 2,
        compiler_params=pltpu.CompilerParams(
            collective_id=1, has_side_effects=True, vmem_limit_bytes=60 * 1024 * 1024
        ),
    )(stokes_q, stokes_u, slab_sums, own_total, highest, lowest)
    farthest = jnp.max(farthest)

    freq = 0.5 + 1.5 * channel_index.astype(jnp.float32) / (NCH - 1)
    lam2 = (0.2998 / freq) ** 2
    weight = 1.0 / (freq * jnp.sqrt(jnp.float32(slab * depth_count)))
    rows = NCH // depth_count

    def by_series(_):
        return pl.pallas_call(
            channel_kernel,
            out_shape=jax.ShapeDtypeStruct((rows, 2, strip, width), jnp.float32),
            in_specs=[smem] * 4 + [vmem] * 2,
            out_specs=vmem,
            compiler_params=params,
        )(
            channel_index,
            lam2,
            weight,
            jnp.asarray(table.reshape(-1)),
            moments,
            faraday_depth,
        )

    def by_sum(_):
        nearer = start + 0.5 * faraday_depth
        whole = pl.BlockSpec((slab, strip, width), lambda c: (0, 0, 0))
        sums = pl.pallas_call(
            direct_kernel,
            grid=(NCH,),
            out_shape=jax.ShapeDtypeStruct((NCH, 2, strip, width), jnp.float32),
            in_specs=[smem] * 2
            + [whole] * 3
            + [pl.BlockSpec((strip, width), lambda c: (0, 0))],
            out_specs=pl.BlockSpec((1, 2, strip, width), lambda c: (c, 0, 0, 0)),
            compiler_params=params,
        )(lam2, weight, stokes_q, stokes_u, slab_sums, nearer)
        sums = sums.reshape(depth_count, rows, 2, strip, width)
        return jnp.sum(lax.all_to_all(sums, "depth", 0, 0), axis=0)

    pol_spectra = lax.cond(farthest <= REACH, by_series, by_sum, 0)
    return (pol_spectra, faraday_depth)


def solution(mesh):
    in_specs = (P(None, "depth", "tile", None), P(), P())
    out_specs = (P("depth", None, "tile", None), P("tile", None))
    return jax.shard_map(body, mesh=mesh, in_specs=in_specs, out_specs=out_specs, check_vma=False)
```

```python
import functools

import jax
import jax.numpy as jnp
import numpy as np
from jax import lax
from jax.experimental import pallas as pl
from jax.experimental.pallas import tpu as pltpu
from jax.sharding import PartitionSpec as P

NCH = 64


two_pi = 6.283185307179586
faraday_coef = 0.25

REACH = 24.0
TERMS = 22


def grid_lam2():
    freq = 0.5 + 1.5 * np.arange(NCH, dtype=np.float64) / (NCH - 1)
    return 2.0 * (0.2998 / freq) ** 2


def series_table():
    lam = grid_lam2()
    middle = 0.5 * (lam.max() + lam.min())
    args = (lam - middle) * REACH
    count = 4096
    theta = (np.arange(count) + 0.5) * (np.pi / count)
    orders = np.arange(TERMS)
    table = np.cos(
        orders[None, :, None] * theta - args[:, None, None] * np.sin(theta)
    ).mean(axis=-1)
    table = table * np.where(orders == 0, 1.0, 2.0)
    table = table * np.where((orders // 2) % 2 == 0, 1.0, -1.0)
    return middle, table.astype(np.float32)


def halves_fit():
    nodes = 0.25 * (np.cos((np.arange(200) + 0.5) * np.pi / 200) + 1.0) / 2.0
    r = np.sqrt(nodes)
    root = np.sqrt(2.0)
    sin_fit = np.polynomial.polynomial.polyfit(nodes, root * np.sin(np.pi * r) / r, 4)
    cos_fit = np.polynomial.polynomial.polyfit(nodes, root * np.cos(np.pi * r), 5)
    return [float(v) for v in sin_fit], [float(v) for v in cos_fit]


SIN_FIT, COS_FIT = halves_fit()


def horner(fit, square):
    total = fit[-1] * square + fit[-2]
    for value in fit[-3::-1]:
        total = total * square + value
    return total


def turn(fraction):
    square = fraction * fraction
    sine = horner(SIN_FIT, square) * fraction
    cosine = horner(COS_FIT, square)
    return 1.0 - sine * sine, sine * cosine


def turn_of_phase(phase):
    laps = jnp.round(phase * (1.0 / two_pi))
    rest = phase - laps * 6.28125
    rest = rest - laps * 0.0019340515136718750
    rest = rest - laps * (two_pi - 6.28125 - 0.0019340515136718750)
    return turn(rest * (1.0 / two_pi))


def field_kernel(
    zcos, pot, zup, zdown, xup, xdown, xcos, ysin,
    q_out, u_out, sum_out, total_out, high_out, low_out,
    zlow, zhigh, xlow, xhigh, send, recv,
):
    slab, strip, width = sum_out.shape
    bands = strip // 8
    barrier = pltpu.get_barrier_semaphore()
    plan = []
    for order, (axis, up, down, low, high) in enumerate(
        (("depth", zup, zdown, zlow, zhigh), ("tile", xup, xdown, xlow, xhigh))
    ):
        place = lax.axis_index(axis)
        last = lax.axis_size(axis) - 1
        above = pltpu.make_async_remote_copy(
            src_ref=up, dst_ref=low, send_sem=send.at[2 * order], recv_sem=recv.at[2 * order],
            device_id={axis: place + 1}, device_id_type=pl.DeviceIdType.MESH,
        )
        below = pltpu.make_async_remote_copy(
            src_ref=down, dst_ref=high, send_sem=send.at[2 * order + 1],
            recv_sem=recv.at[2 * order + 1],
            device_id={axis: place - 1}, device_id_type=pl.DeviceIdType.MESH,
        )
        plan.append((axis, place, last, above, below, low, high))

    def signal(axis, index):
        pl.semaphore_signal(
            barrier, inc=1, device_id={axis: index}, device_id_type=pl.DeviceIdType.MESH
        )

    count = 0
    for axis, place, last, above, below, low, high in plan:
        pl.when(place > 0)(functools.partial(signal, axis, place - 1))
        pl.when(place < last)(functools.partial(signal, axis, place + 1))
        count = count + (place + last - 1) // last + (2 * last - place - 1) // last
    pl.semaphore_wait(barrier, count)
    for axis, place, last, above, below, low, high in plan:
        pl.when(place < last)(above.start)
        pl.when(place > 0)(below.start)
    for axis, place, last, above, below, low, high in plan:

        @pl.when(place == 0)
        def _():
            low[...] = jnp.zeros_like(low)

        @pl.when(place == last)
        def _():
            high[...] = jnp.zeros_like(high)

    def arrive(axis, place, last, above, below, low, high):
        @pl.when(place < last)
        def _():
            above.wait_send()
            below.wait_recv()

        @pl.when(place > 0)
        def _():
            below.wait_send()
            above.wait_recv()

    column = lax.broadcasted_iota(jnp.int32, (8, width), 1)

    def along_last(v):
        up1 = jnp.where(column < width - 1, pltpu.roll(v, width - 1, 1), 0.0)
        up2 = jnp.where(column < width - 2, pltpu.roll(v, width - 2, 1), 0.0)
        down1 = jnp.where(column >= 1, pltpu.roll(v, 1, 1), 0.0)
        down2 = jnp.where(column >= 2, pltpu.roll(v, 2, 1), 0.0)
        return (8.0 * (up1 - down1) - (up2 - down2)) * (1.0 / 12.0)

    def one_band(band):
        rows = slice(8 * band, 8 * band + 8)
        ybase = jnp.broadcast_to(1.0 + 0.3 * ysin[...], (8, width))
        xhalf = jnp.broadcast_to(0.5 * xcos[rows], (8, width))

        def pair_of(ref, component, z):
            return jnp.concatenate([ref[component, k, pl.ds(z, 1)] for k in range(2)], axis=0)

        def along_mid(component, z):
            if band == 0:
                v = jnp.concatenate(
                    [pair_of(xlow, component - 1, z), pot[component, z, 0:16]], axis=0
                )
                at = 0
            elif band == bands - 1:
                v = jnp.concatenate(
                    [pot[component, z, strip - 16 : strip], pair_of(xhigh, component - 1, z)], axis=0
                )
                at = 6
            else:
                v = pot[component, z, 8 * band - 8 : 8 * band + 16]
                at = 6
            return (
                8.0 * (v[at + 3 : at + 11] - v[at + 1 : at + 9])
                - (v[at + 4 : at + 12] - v[at : at + 8])
            ) * (1.0 / 12.0)

        def along_lead(component, z, edge):
            def plane(step):
                if edge is None:
                    return pot[component, z + step, rows]
                place = edge + step
                if place < 0:
                    return zlow[component, place + 2, rows]
                if place >= slab:
                    return zhigh[component, place - slab, rows]
                return pot[component, place, rows]

            return (8.0 * (plane(1) - plane(-1)) - (plane(2) - plane(-2))) * (1.0 / 12.0)

        def one(z, state, edge=None):
            before, high, low = state
            field_x = along_last(pot[2, z, rows]) - along_lead(1, z, edge)
            field_y = along_lead(0, z, edge) - along_mid(2, z)
            field_z = along_mid(1, z) - along_last(pot[0, z, rows])
            density = ybase + zcos[z] * xhalf
            q_out[z, rows] = density * (field_y * field_y - field_x * field_x)
            u_out[z, rows] = -2.0 * density * field_x * field_y
            now = before + density * field_z
            sum_out[z, rows] = now
            return now, jnp.maximum(high, now), jnp.minimum(low, now)

        zero = jnp.zeros((8, width), jnp.float32)
        state = (zero, zero, zero)
        for z in (0, 1):
            state = one(z, state, z)
        state = lax.fori_loop(2, slab - 2, one, state)
        for z in (slab - 2, slab - 1):
            state = one(z, state, z)
        total_out[rows] = faraday_coef * state[0]
        high_out[rows] = faraday_coef * state[1]
        low_out[rows] = faraday_coef * state[2]

    arrive(*plan[0])
    for band in range(1, bands - 1):
        one_band(band)
    arrive(*plan[1])
    for band in (0, bands - 1):
        one_band(band)


def moment_kernel(
    middle, q_ref, u_ref, sum_ref, total_ref, high_ref, low_ref,
    out, depth_out, far_out, start_ref,
    others, own, near, part, across, far, far_depth, far_mid, far_tile,
    carry_send, carry_recv, far_send, far_recv, tile_send, tile_recv,
    near_send, near_recv, cross_send, cross_recv, back_send, back_recv,
):
    slab, strip, width = sum_ref.shape
    group = 8 if slab % 8 == 0 else 1
    chunks = strip // 8
    depth_count, tile_count = lax.axis_size("depth"), lax.axis_size("tile")
    depth_place, tile_place = lax.axis_index("depth"), lax.axis_index("tile")
    core = lax.rem(depth_place, 2)
    chip_count = depth_count // 2
    chip = depth_place // 2
    partner = depth_place + 1 - 2 * core

    def copy(src, dst, send, recv, axis, index):
        return pltpu.make_async_remote_copy(
            src_ref=src, dst_ref=dst, send_sem=send, recv_sem=recv,
            device_id={axis: index}, device_id_type=pl.DeviceIdType.MESH,
        )

    def depth_peer(k):
        return lax.rem(depth_place + k, depth_count)

    def tile_peer(k):
        return lax.rem(tile_place + k, tile_count)

    barrier = pltpu.get_barrier_semaphore()
    for k in range(1, depth_count):
        pl.semaphore_signal(
            barrier, inc=1, device_id={"depth": depth_peer(k)},
            device_id_type=pl.DeviceIdType.MESH,
        )
    for k in range(1, tile_count):
        pl.semaphore_signal(
            barrier, inc=1, device_id={"tile": tile_peer(k)},
            device_id_type=pl.DeviceIdType.MESH,
        )
    pl.semaphore_wait(barrier, depth_count + tile_count - 2)

    carries = [
        copy(total_ref, others.at[k - 1], carry_send.at[k - 1], carry_recv.at[k - 1],
             "depth", depth_peer(k))
        for k in range(1, depth_count)
    ]
    for item in carries:
        item.start()
    for item in carries:
        item.wait()
    nearer = jnp.zeros((strip, width), jnp.float32)
    whole = total_ref[...]
    for k in range(1, depth_count):
        part_k = others[k - 1]
        whole = whole + part_k
        nearer = nearer + jnp.where(depth_place >= k, part_k, 0.0)
    depth_out[...] = whole
    start = nearer - 0.5 * whole
    start_ref[...] = start
    reach = jnp.maximum(jnp.abs(high_ref[...] + start), jnp.abs(low_ref[...] + start))
    reach = functools.reduce(
        jnp.maximum, [reach[:, k * 128 : (k + 1) * 128] for k in range(width // 128)]
    )
    far[...] = functools.reduce(jnp.maximum, [reach[k * 8 : k * 8 + 8] for k in range(chunks)])
    fars = [
        copy(far, far_depth.at[k - 1], far_send.at[k - 1], far_recv.at[k - 1],
             "depth", depth_peer(k))
        for k in range(1, depth_count)
    ]
    for item in fars:
        item.start()

    def tile(row, col, g):
        rows = pl.ds(pl.multiple_of(row, 8), 8)
        cols = pl.ds(pl.multiple_of(col, 128), 128)
        place = (rows, cols)
        start = start_ref[place]
        for half in range(2):
            for j in range(TERMS):
                own[g, half, j, :, cols] = jnp.zeros((8, 128), jnp.float32)

        def block(step, carry):
            q_prev, q_now, u_prev, u_now, twice = [], [], [], [], []
            for k in range(group):
                z = step * group + k
                shift = faraday_coef * sum_ref[(z,) + place] + start
                laps = shift * (middle / two_pi)
                cosine, sine = turn(laps - jnp.round(laps))
                q = q_ref[(z,) + place]
                u = u_ref[(z,) + place]
                x = shift * (1.0 / REACH)
                q_prev.append(q * cosine - u * sine)
                u_prev.append(q * sine + u * cosine)
                twice.append(x + x)
                q_now.append(x * q_prev[-1])
                u_now.append(x * u_prev[-1])
            own[g, 0, 0, :, cols] += functools.reduce(jnp.add, q_prev)
            own[g, 1, 0, :, cols] += functools.reduce(jnp.add, u_prev)
            for j in range(1, TERMS):
                own[g, 0, j, :, cols] += functools.reduce(jnp.add, q_now)
                own[g, 1, j, :, cols] += functools.reduce(jnp.add, u_now)
                if j < TERMS - 1:
                    for k in range(group):
                        q_prev[k], q_now[k] = q_now[k], twice[k] * q_now[k] - q_prev[k]
                        u_prev[k], u_now[k] = u_now[k], twice[k] * u_now[k] - u_prev[k]
            return carry

        lax.fori_loop(0, slab // group, block, 0)

    def near_copy(g):
        return copy(own.at[g, 1 - core], near.at[g], near_send.at[g], near_recv.at[g],
                    "depth", partner)

    def cross_copies(g):
        return [
            copy(part.at[g], across.at[g, k - 1], cross_send.at[g, k - 1],
                 cross_recv.at[g, k - 1], "depth", 2 * lax.rem(chip + k, chip_count) + core)
            for k in range(1, chip_count)
        ]

    def back_copy(g):
        piece = out.at[core, :, pl.ds(pl.multiple_of(g * 8, 8), 8)]
        return copy(piece, piece, back_send.at[g], back_recv.at[g], "depth", partner)

    def compute(g):
        lax.fori_loop(
            0, width // 128, lambda c, carry: (tile(g * 8, c * 128, g), carry)[1], 0
        )
        near_copy(g).start()

    def sum_chip(g):
        near_copy(g).wait()
        part[g] = own[g, core] + near[g]
        for item in cross_copies(g):
            item.start()

    def sum_all(g):
        total = part[g]
        for k, item in enumerate(cross_copies(g)):
            item.wait()
            total = total + across[g, k]
        out[core, :, pl.ds(pl.multiple_of(g * 8, 8), 8)] = total
        back_copy(g).start()

    tiles_far = [
        copy(far_mid, far_tile.at[k - 1], tile_send.at[k - 1], tile_recv.at[k - 1],
             "tile", tile_peer(k))
        for k in range(1, tile_count)
    ]

    def lap(g, carry):
        pl.when(g < chunks)(lambda: compute(g))

        @pl.when(g == 0)
        def _():
            reach = far[...]
            for k, item in enumerate(fars):
                item.wait()
                reach = jnp.maximum(reach, far_depth[k])
            far_mid[...] = reach
            for item in tiles_far:
                item.start()

        pl.when(g < chunks)(lambda: sum_chip(g))
        pl.when(g >= 1)(lambda: sum_all(g - 1))
        return carry

    lax.fori_loop(0, chunks + 1, lap, 0)
    reach = far_mid[...]
    for k, item in enumerate(tiles_far):
        item.wait()
        reach = jnp.maximum(reach, far_tile[k])
    far_out[...] = reach
    for g in range(chunks):
        back_copy(g).wait()


def channel_kernel(index, lam, weight, table, moments, depth_ref, out):
    rows, _, strip, width = out.shape
    first_row = lax.axis_index("depth") * rows

    def band(step, carry):
        place = pl.ds(pl.multiple_of(step * 8, 8), 8)
        half = 0.5 * depth_ref[place]

        def one(row, carry):
            base = index[first_row + row] * TERMS
            real_part = table[base] * moments[0, 0, place]
            imag_part = table[base] * moments[1, 0, place]
            for j in range(1, TERMS):
                factor = table[base + j]
                first = factor * moments[0, j, place]
                second = factor * moments[1, j, place]
                if j % 2 == 0:
                    real_part = real_part + first
                    imag_part = imag_part + second
                else:
                    real_part = real_part - second
                    imag_part = imag_part + first
            cosine, sine = turn_of_phase(2.0 * lam[first_row + row] * half)
            out[row, 0, place] = (real_part * cosine - imag_part * sine) * weight[first_row + row]
            out[row, 1, place] = (real_part * sine + imag_part * cosine) * weight[first_row + row]
            return carry

        return lax.fori_loop(0, rows, one, carry)

    lax.fori_loop(0, strip // 8, band, 0)


def direct_kernel(lam, weight, q_ref, u_ref, sum_ref, nearer_ref, out):
    slab, strip, width = sum_ref.shape
    twice = 2.0 * lam[pl.program_id(0)]
    scale = weight[pl.program_id(0)]

    def band(step, carry):
        place = pl.ds(pl.multiple_of(step * 8, 8), 8)
        nearer = nearer_ref[place]

        def one(z, sums):
            cosine, sine = turn_of_phase(twice * (faraday_coef * sum_ref[z, place] + nearer))
            q = q_ref[z, place]
            u = u_ref[z, place]
            return sums[0] + (q * cosine - u * sine), sums[1] + (q * sine + u * cosine)

        zero = jnp.zeros((8, width), jnp.float32)
        real_part, imag_part = lax.fori_loop(0, slab, one, (zero, zero))
        out[0, 0, place] = real_part * scale
        out[0, 1, place] = imag_part * scale
        return carry

    lax.fori_loop(0, strip // 8, band, 0)


vmem = pl.BlockSpec(memory_space=pltpu.VMEM)
smem = pl.BlockSpec(memory_space=pltpu.SMEM)
params = pltpu.CompilerParams(vmem_limit_bytes=60 * 1024 * 1024)


def body(potential, channel_index, patch_offsets):
    depth_count = lax.axis_size("depth")
    depth_place = lax.axis_index("depth")
    slab, strip, width = (potential.shape[1], potential.shape[2], potential.shape[3])
    shapes = [(2, 2, strip, width)] * 2 + [(2, 2, slab, width)] * 2
    zstart = depth_place * slab
    xstart = lax.axis_index("tile") * strip
    zpos = (zstart + jnp.arange(slab, dtype=jnp.int32) + patch_offsets[0]).astype(jnp.float32)
    xpos = (xstart + jnp.arange(strip, dtype=jnp.int32) + patch_offsets[1]).astype(jnp.float32)
    ypos = (jnp.arange(width, dtype=jnp.int32) + patch_offsets[2]).astype(jnp.float32)
    zcos = jnp.cos(zpos * (two_pi / 61.0))
    xcos = jnp.cos(xpos * (two_pi / 37.0))[:, None]
    ysin = jnp.sin(ypos * (two_pi / 53.0))[None, :]
    plane = jax.ShapeDtypeStruct((slab, strip, width), jnp.float32)
    flat = jax.ShapeDtypeStruct((strip, width), jnp.float32)
    stokes_q, stokes_u, slab_sums, own_total, highest, lowest = pl.pallas_call(
        field_kernel,
        out_shape=(plane, plane, plane, flat, flat, flat),
        in_specs=[smem] + [vmem] * 7,
        out_specs=(vmem,) * 6,
        scratch_shapes=[pltpu.VMEM(shape, jnp.float32) for shape in shapes]
        + [pltpu.SemaphoreType.DMA((4,))] * 2,
        compiler_params=pltpu.CompilerParams(
            collective_id=0, has_side_effects=True, vmem_limit_bytes=60 * 1024 * 1024
        ),
    )(
        zcos,
        potential,
        potential[0:2, slab - 2 :],
        potential[0:2, :2],
        potential[1:3, :, strip - 2 :].transpose(0, 2, 1, 3),
        potential[1:3, :, :2].transpose(0, 2, 1, 3),
        xcos,
        ysin,
    )

    middle, table = series_table()
    tile_count = lax.axis_size("tile")
    chunks, chip_count = strip // 8, depth_count // 2
    half = (TERMS, 8, width)
    small = (8, 128)
    dma = pltpu.SemaphoreType.DMA
    pair = [dma((depth_count - 1,))] * 4 + [dma((tile_count - 1,))] * 2
    moments, faraday_depth, farthest, start = pl.pallas_call(
        functools.partial(moment_kernel, float(middle)),
        out_shape=(
            jax.ShapeDtypeStruct((2, TERMS, strip, width), jnp.float32),
            flat,
            jax.ShapeDtypeStruct(small, jnp.float32),
            flat,
        ),
        in_specs=[vmem] * 6,
        out_specs=(vmem,) * 4,
        scratch_shapes=[
            pltpu.VMEM((depth_count - 1, strip, width), jnp.float32),
            pltpu.VMEM((chunks, 2) + half, jnp.float32),
            pltpu.VMEM((chunks,) + half, jnp.float32),
            pltpu.VMEM((chunks,) + half, jnp.float32),
            pltpu.VMEM((chunks, chip_count - 1) + half, jnp.float32),
            pltpu.VMEM(small, jnp.float32),
            pltpu.VMEM((depth_count - 1,) + small, jnp.float32),
            pltpu.VMEM(small, jnp.float32),
            pltpu.VMEM((tile_count - 1,) + small, jnp.float32),
        ]
        + pair
        + [dma((chunks,))] * 2
        + [dma((chunks, chip_count - 1))] * 2
        + [dma((chunks,))] * 2,
        compiler_params=pltpu.CompilerParams(
            collective_id=1, has_side_effects=True, vmem_limit_bytes=60 * 1024 * 1024
        ),
    )(stokes_q, stokes_u, slab_sums, own_total, highest, lowest)
    farthest = jnp.max(farthest)

    freq = 0.5 + 1.5 * channel_index.astype(jnp.float32) / (NCH - 1)
    lam2 = (0.2998 / freq) ** 2
    weight = 1.0 / (freq * jnp.sqrt(jnp.float32(slab * depth_count)))
    rows = NCH // depth_count

    def by_series(_):
        return pl.pallas_call(
            channel_kernel,
            out_shape=jax.ShapeDtypeStruct((rows, 2, strip, width), jnp.float32),
            in_specs=[smem] * 4 + [vmem] * 2,
            out_specs=vmem,
            compiler_params=params,
        )(
            channel_index,
            lam2,
            weight,
            jnp.asarray(table.reshape(-1)),
            moments,
            faraday_depth,
        )

    def by_sum(_):
        nearer = start + 0.5 * faraday_depth
        whole = pl.BlockSpec((slab, strip, width), lambda c: (0, 0, 0))
        sums = pl.pallas_call(
            direct_kernel,
            grid=(NCH,),
            out_shape=jax.ShapeDtypeStruct((NCH, 2, strip, width), jnp.float32),
            in_specs=[smem] * 2
            + [whole] * 3
            + [pl.BlockSpec((strip, width), lambda c: (0, 0))],
            out_specs=pl.BlockSpec((1, 2, strip, width), lambda c: (c, 0, 0, 0)),
            compiler_params=params,
        )(lam2, weight, stokes_q, stokes_u, slab_sums, nearer)
        sums = sums.reshape(depth_count, rows, 2, strip, width)
        return jnp.sum(lax.all_to_all(sums, "depth", 0, 0), axis=0)

    pol_spectra = lax.cond(farthest <= REACH, by_series, by_sum, 0)
    return (pol_spectra, faraday_depth)


def solution(mesh):
    in_specs = (P(None, "depth", "tile", None), P(), P())
    out_specs = (P("depth", None, "tile", None), P("tile", None))
    return jax.shard_map(body, mesh=mesh, in_specs=in_specs, out_specs=out_specs, check_vma=False)
```
